128 devices in a mesh: atom: 8 (over x, core), aux: 16 (over z, y).
Axes of the slice: x: 4, y: 4, z: 4, core: 2. Of those that a mesh axis runs over, the one named last changes fastest.
Arguments:
- three_index: bfloat16 [256, 16, 4, 128, 128], P('aux', 'atom'), may hold values from -0.09375 to 0.09375
- density: bfloat16 [2048, 2048], P(('atom', 'aux')), may hold values from -6 to 6
- pair_blocks: int32 [16, 4], replicated, may hold values from 0 to 15, as said below
- basis_counts: int32 [16], replicated, may hold values from 1 to 128, 1536 in all
Outputs:
- exchange_matrix: float32 [2048, 2048], P(('atom', 'aux'))
The draws below stay inside these ranges and needn't reach their ends.
Inputs may be any that keep to these rules, and one draw needn't show every extreme that they name: `pair_blocks`: each row names 4 different basis blocks, the first being the row's own block.
All inputs are finite; a program needn't handle non-finite values.
Results may differ from the reference program's by a relative error of at most 0.0029.
Values may be sent and summed in bfloat16 or wider, within the bound.
No kernel may reach another device: no remote copies, remote signals or barrier semaphores. Data moves between devices by JAX's collectives and lax.ppermute only.
A program may use at most 192 MiB of HBM per device.

```python
import math
import jax
import jax.numpy as jnp
import numpy as np
from jax import lax

BS = 128
NAB = 1
NEIGH = 4
NBLK = 16
NBF = 2048
AUXW = 256


def draw_pair_blocks(key, part):
    scores = jax.random.randint(key, (NBLK, NBLK), 0, 1 << 20)
    indices = jnp.arange(NBLK)
    scores = scores * NBLK + indices[None, :]
    scores = jnp.where(indices[:, None] == indices[None, :], -1, scores)
    ordering = jnp.argsort(scores, axis=1, stable=True)
    return ordering[:, :NEIGH].astype(jnp.int32)


def shard_levels(rng, dims, shards, smallest, largest):
    factor_of = 1.0
    for position, parts in shards:
        steps = jax.random.uniform(jax.random.fold_in(jax.random.fold_in(rng, 6), position), (parts,), jnp.float32, smallest / len(shards), largest / len(shards))
        factor_of = factor_of * jnp.repeat(jnp.exp(steps), dims[position] // parts).reshape((-1,) + (1,) * (len(dims) - 1 - position))
    return factor_of


def split_up(number_of, total, reach, slope):
    portions = [(1 << 20) // math.isqrt(rank ** slope) + 1 for rank in range(2, number_of + 1)]
    surplus, holding = total - reach - (number_of - 1), [1] * (number_of - 1)
    while surplus > 0:
        free = [i for i in range(number_of - 1) if holding[i] < reach]
        whole, remaining = sum([portions[i] for i in free]), surplus
        for i in free:
            more = min(reach - holding[i], max(1, remaining * portions[i] // whole), surplus)
            holding[i] = holding[i] + more
            surplus = surplus - more
    return np.array([reach] + holding)


def ragged(rng, amount, total, bound, slope):
    if amount == 2:
        one = jax.random.randint(rng, (), max(1, total - bound), min(bound, total - 1) + 1)
        return jnp.stack([one, total - one])
    lengths = jnp.asarray(split_up(amount, total, bound, slope), jnp.int32)
    couples = (amount - 1) // 2
    donor, receiver = lengths[1:1 + 2 * couples:2], lengths[2:2 + 2 * couples:2]
    slack = jnp.minimum(donor - 1, bound - receiver)
    shifted = jax.random.randint(jax.random.fold_in(rng, 1), (couples,), 0, 1 << 20) % (slack + 1)
    lengths = lengths.at[1:1 + 2 * couples:2].set(donor - shifted).at[2:2 + 2 * couples:2].set(receiver + shifted)
    return lengths[jax.random.permutation(jax.random.fold_in(rng, 2), amount)]


def gaussian(own_key, extent, width, reach, shards=(), kind=jnp.bfloat16):
    loudness = shard_levels(own_key, extent, shards, -0.22, 0.18) if shards else 1.0
    array = jax.random.normal(own_key, extent, jnp.float32) * width * loudness
    return jnp.minimum(jnp.maximum(array, -reach), reach).astype(kind)


def setup_inputs(seed: int = 0) -> dict:
    keys = jax.random.split(jax.random.key(seed), 5)
    return {
        "three_index": gaussian(keys[0], (AUXW, NBLK, NEIGH, BS, BS), (NEIGH * BS * 8 * NAB) ** -0.5, 0.09375, ((0, 16), (1, 8))),
        "density": gaussian(keys[1], (NBF, NBF), 1.0, 6.0, ((0, 128),)),
        "pair_blocks": draw_pair_blocks(jax.random.fold_in(keys[4], 71), 0),
        "basis_counts": ragged(keys[3], NBLK, NBLK * BS * 3 // 4, BS, 2).astype(jnp.int32),
    }


def reference(three_index, density, pair_blocks, basis_counts):
    live_slots = (jnp.arange(BS)[None, :] < basis_counts[:, None]).astype(jnp.bfloat16)
    col_live = live_slots[pair_blocks]
    masked = three_index * live_slots[None, :, None, :, None] * col_live[None, :, :, None, :]
    near_density = density.reshape(NBLK, BS, NBF)[pair_blocks]
    placement = (pair_blocks.reshape(-1)[:, None] == jnp.arange(NBLK)[None, :]).astype(jnp.float32)
    group_size = math.gcd(AUXW, 8)
    grouped = masked.reshape(AUXW // group_size, group_size, NBLK, NEIGH, BS, BS)

    def advance(running, portion):
        halfway = jnp.einsum('pmjab,mjbs->pmas', portion.astype(jnp.float32), near_density.astype(jnp.float32))
        halfway = halfway.astype(jnp.bfloat16).reshape(group_size, NBF, NBLK, BS)
        contrib = jnp.einsum('pmbc,pbjcn->mbjn', halfway.astype(jnp.float32), portion.astype(jnp.float32))
        spread_out = jnp.einsum('mqn,qk->mkn', contrib.reshape(NBF, NBLK * NEIGH, BS), placement,
                                precision=lax.Precision.HIGHEST)
        return running + spread_out.reshape(NBF, NBF), None

    running, _ = lax.scan(advance, jnp.zeros((NBF, NBF), jnp.float32), grouped)
    return running
```

```python
import functools

import jax
import jax.numpy as jnp
from jax import lax
from jax.experimental import pallas as pl
from jax.experimental.pallas import tpu as pltpu
from jax.sharding import Mesh, PartitionSpec as P

CORES = 2
SIDE = 4


def exchange_kernel(groups, place, pairs, own_hbm, other_hbm, density_hbm, out_ref,
                    own, other, density, halfway, total, sems):
    sources, aux, per_source, neigh, size, _ = own.shape
    tiles, basis, width = density.shape
    step = pl.program_id(0)
    core = place[0]

    copies = [pltpu.make_async_copy(own_hbm, own, sems.at[0])]
    for t in range(tiles):
        copies.append(
            pltpu.make_async_copy(
                density_hbm.at[:, pl.ds(t * width, width)], density.at[t], sems.at[1 + t]
            )
        )
    copies.append(pltpu.make_async_copy(other_hbm, other, sems.at[1 + tiles]))

    @pl.when(step == 0)
    def _():
        for copy in copies:
            copy.start()
        copies[0].wait()

    blocks_here = halfway.shape[1] // size
    per_group = blocks_here // per_source

    for t in range(tiles):
        @pl.when(step == 0)
        def _():
            copies[1 + t].wait()

        @pl.loop(0, blocks_here)
        def _(b):
            source = step * per_group + b // per_source
            mi = b % per_source
            block = (source * CORES + core) * per_source + mi
            rows = jnp.concatenate(
                [
                    jnp.concatenate([own[source, p, mi, j] for j in range(neigh)], axis=1)
                    for p in range(aux)
                ],
                axis=0,
            )
            near = jnp.concatenate(
                [
                    density[t, pl.ds(pl.multiple_of(pairs[block * neigh + j] * size, size), size), :]
                    for j in range(neigh)
                ],
                axis=0,
            )
            product = jnp.dot(rows, near, preferred_element_type=jnp.float32).astype(jnp.bfloat16)
            at = pl.ds(pl.multiple_of(b * size, size), size)
            for k in range(width // size):
                for p in range(aux):
                    halfway[t * (width // size) + k, at, p * size : (p + 1) * size] = product[
                        p * size : (p + 1) * size, k * size : (k + 1) * size
                    ]

    @pl.when(step == 0)
    def _():
        copies[-1].wait()

    total[...] = jnp.zeros_like(total)

    def add_in(tensor, which):
        @pl.loop(0, sources * per_source)
        def _(b):
            source = b // per_source
            mi = b % per_source
            block = (source * CORES + which) * per_source + mi
            rows = jnp.concatenate(
                [
                    jnp.concatenate([tensor[source, p, mi, j] for j in range(neigh)], axis=1)
                    for p in range(aux)
                ],
                axis=0,
            )
            product = jnp.dot(halfway[block], rows, preferred_element_type=jnp.float32)
            for j in range(neigh):
                total[pairs[block * neigh + j]] += product[:, j * size : (j + 1) * size]

    add_in(own, core)
    add_in(other, 1 - core)
    for n in range(basis // size):
        out_ref[:, n * size : (n + 1) * size] = total[n].astype(out_ref.dtype)


def exchange_rows(place, pairs, own, other, density, groups=2, tiles=4):
    sources, aux, per_source, neigh, size, _ = own.shape
    basis = density.shape[0]
    rows = sources * per_source * size
    return pl.pallas_call(
        functools.partial(exchange_kernel, groups),
        out_shape=jax.ShapeDtypeStruct((rows, basis), jnp.bfloat16),
        grid_spec=pltpu.PrefetchScalarGridSpec(
            num_scalar_prefetch=2,
            grid=(groups,),
            in_specs=[pl.BlockSpec(memory_space=pl.ANY)] * 3,
            out_specs=pl.BlockSpec((rows // groups, basis), lambda g, *_: (g, 0)),
            scratch_shapes=[
                pltpu.VMEM(own.shape, jnp.bfloat16),
                pltpu.VMEM(own.shape, jnp.bfloat16),
                pltpu.VMEM((tiles, basis, basis // tiles), jnp.bfloat16),
                pltpu.VMEM((basis // size, rows // groups, aux * size), jnp.bfloat16),
                pltpu.VMEM((basis // size, rows // groups, size), jnp.float32),
                pltpu.SemaphoreType.DMA((tiles + 2,)),
            ],
        ),
        compiler_params=pltpu.CompilerParams(
            vmem_limit_bytes=56 << 20, dimension_semantics=("arbitrary",)
        ),
        cost_estimate=pl.CostEstimate(
            flops=4 * rows * aux * neigh * size * basis,
            bytes_accessed=4 * own.size + 2 * density.size + 2 * rows * basis,
            transcendentals=0,
        ),
    )(place, pairs, own, other, density)


def per_device(three_index, density, pair_blocks, basis_counts):
    aux_here, own_blocks, neigh, size, _ = three_index.shape
    rows_here, basis = density.shape
    blocks = basis // size
    x, core = lax.axis_index("x"), lax.axis_index("core")
    zy = lax.axis_index("z") * lax.axis_size("y") + lax.axis_index("y")
    first_row = (x * CORES + core) * own_blocks * size + zy * rows_here

    column_live = (jnp.arange(size)[None, :] < basis_counts[:, None]).reshape(basis)
    row_numbers = first_row % size + jnp.arange(rows_here)
    row_live = row_numbers < basis_counts[first_row // size]
    live = row_live[:, None] & column_live[None, :]

    kept = jnp.where(live, density, 0)
    whole = lax.all_gather(kept, ("x", "core", "z", "y"), axis=0, tiled=True)

    parted = three_index.reshape(SIDE, aux_here // SIDE, own_blocks, neigh, size, size)
    own = lax.all_to_all(parted, "x", 0, 0, tiled=True)
    other = lax.ppermute(own, "core", [(0, 1), (1, 0)])

    place = core.astype(jnp.int32).reshape(1)
    partial = exchange_rows(place, pair_blocks.reshape(-1), own, other, whole)
    pieces = lax.all_to_all(partial.reshape(-1, rows_here, basis), ("x", "z", "y"), 0, 0, tiled=True)
    summed = jnp.sum(pieces.astype(jnp.float32), axis=0)
    return jnp.where(live, summed, 0)


def solution(mesh):
    devices = mesh.devices.reshape(SIDE, CORES, SIDE, SIDE)
    fine = Mesh(devices, ("x", "core", "z", "y"))
    in_specs = (P(("z", "y"), ("x", "core")), P(("x", "core", "z", "y"), None), P(), P())
    out_specs = P(("x", "core", "z", "y"), None)
    return jax.shard_map(
        per_device, mesh=fine, in_specs=in_specs, out_specs=out_specs, check_vma=False
    )
```

```python
import jax
import jax.numpy as jnp
from jax import lax
from jax.experimental import pallas as pl
from jax.experimental.pallas import tpu as pltpu
from jax.sharding import Mesh, PartitionSpec as P

CORES = 2
SIDE = 4
LIVE = 1536
LANES = 128
PIECE = 128
WIDTH = 1024


def stacked(tensor, source, mi, aux, neigh):
    return jnp.concatenate(
        [
            jnp.concatenate([tensor[source, p, mi, j] for j in range(neigh)], axis=1)
            for p in range(aux)
        ],
        axis=0,
    )


def exchange_kernel(place, pairs, starts, shifts, counts, own_hbm, other_hbm, density_hbm,
                    out_ref, own, other, density, halfway, total, sems):
    sources, aux, per_source, neigh, size, _ = own.shape
    tiles, basis, width = density.shape
    rows = sources * per_source * size
    core = place[0]

    own_copy = pltpu.make_async_copy(own_hbm, own, sems.at[0])
    other_copy = pltpu.make_async_copy(other_hbm, other, sems.at[1])
    density_copies = [
        pltpu.make_async_copy(
            density_hbm.at[:, t * width : (t + 1) * width], density.at[t], sems.at[2 + t]
        )
        for t in range(tiles)
    ]
    own_copy.start()
    density_copies[0].start()
    own_copy.wait()

    for t in range(tiles):
        density_copies[t].wait()
        if t + 1 < tiles:
            density_copies[t + 1].start()
        if t == 0:
            other_copy.start()

        def first(b, carry):
            block = (b // per_source * CORES + core) * per_source + b % per_source
            at = pl.ds(pl.multiple_of(b * size, size), size)
            lhs = stacked(own, b // per_source, b % per_source, aux, neigh)
            near = jnp.concatenate(
                [
                    density[t, pl.ds(pl.multiple_of(pairs[block * neigh + j] * size, size), size), :]
                    for j in range(neigh)
                ],
                axis=0,
            )
            product = jnp.dot(lhs, near, preferred_element_type=jnp.float32).astype(jnp.bfloat16)
            for k in range(width // size):
                for p in range(aux):
                    halfway[t * (width // size) + k, at, p * size : (p + 1) * size] = product[
                        p * size : (p + 1) * size, k * size : (k + 1) * size
                    ]
            return carry

        lax.fori_loop(0, sources * per_source, first, 0, unroll=2)

    total[...] = jnp.zeros_like(total)
    other_copy.wait()

    def add_in(tensor, which):
        def second(b, carry):
            block = (b // per_source * CORES + which) * per_source + b % per_source
            rhs = stacked(tensor, b // per_source, b % per_source, aux, neigh)
            for r in range(0, rows, PIECE):
                product = jnp.dot(
                    halfway[block, r : r + PIECE], rhs, preferred_element_type=jnp.float32
                )
                for j in range(neigh):
                    total[pairs[block * neigh + j], r : r + PIECE] += product[
                        :, j * size : (j + 1) * size
                    ]
            return carry

        lax.fori_loop(0, sources * per_source, second, 0, unroll=2)

    add_in(own, core)
    add_in(other, 1 - core)

    out_ref[...] = jnp.zeros_like(out_ref)
    row = lax.broadcasted_iota(jnp.int32, (size, 2 * LANES), 0)
    column = lax.broadcasted_iota(jnp.int32, (size, 2 * LANES), 1)

    def pack(n, carry):
        chosen = (column == row + shifts[n]) & (row < counts[n])
        moved = jnp.dot(
            total[n].astype(jnp.bfloat16),
            jnp.where(chosen, 1.0, 0.0).astype(jnp.bfloat16),
            preferred_element_type=jnp.float32,
        ).astype(jnp.bfloat16)
        at = pl.ds(pl.multiple_of(starts[n] * LANES, LANES), 2 * LANES)
        out_ref[:, at] += moved
        return carry

    lax.fori_loop(0, basis // size, pack, 0)


def exchange_rows(place, pairs, starts, shifts, counts, own, other, density):
    sources, aux, per_source, neigh, size, _ = own.shape
    basis = density.shape[0]
    rows = sources * per_source * size
    scalar, vector = pl.BlockSpec(memory_space=pltpu.SMEM), pl.BlockSpec(memory_space=pltpu.VMEM)
    tiles = basis // WIDTH
    return pl.pallas_call(
        exchange_kernel,
        out_shape=jax.ShapeDtypeStruct((rows, LIVE), jnp.bfloat16),
        in_specs=[scalar] * 5 + [pl.BlockSpec(memory_space=pl.ANY)] * 3,
        out_specs=vector,
        scratch_shapes=[
            pltpu.VMEM(own.shape, jnp.bfloat16),
            pltpu.VMEM(own.shape, jnp.bfloat16),
            pltpu.VMEM((tiles, basis, WIDTH), jnp.bfloat16),
            pltpu.VMEM((basis // size, rows, aux * size), jnp.bfloat16),
            pltpu.VMEM((basis // size, rows, size), jnp.float32),
            pltpu.SemaphoreType.DMA((2 + tiles,)),
        ],
        compiler_params=pltpu.CompilerParams(vmem_limit_bytes=52 << 20),
        cost_estimate=pl.CostEstimate(
            flops=4 * rows * aux * neigh * size * basis,
            bytes_accessed=4 * own.size + 2 * density.size + 2 * rows * LIVE,
            transcendentals=0,
        ),
    )(place, pairs, starts, shifts, counts, own, other, density)


def finish_kernel(rows_live, starts, shifts, counts, pieces, out_ref, summed):
    amount, rows, _ = pieces.shape
    summed[...] = jnp.zeros_like(summed)

    def add(i, carry):
        part = pieces[pl.ds(i * 8, 8)].astype(jnp.float32)
        summed[...] += jnp.sum(part, axis=0)
        return carry

    lax.fori_loop(0, amount // 8, add, 0)
    row = lax.broadcasted_iota(jnp.int32, (rows, LANES), 0)
    lane = lax.broadcasted_iota(jnp.int32, (rows, LANES), 1)
    for n in range(out_ref.shape[1] // LANES):
        window = summed[:, pl.ds(pl.multiple_of(starts[n] * LANES, LANES), 2 * LANES)]
        turned = pltpu.roll(window, lax.rem(2 * LANES - shifts[n], 2 * LANES), axis=1)
        live = (lane < counts[n]) & (row < rows_live[0])
        out_ref[:, n * LANES : (n + 1) * LANES] = jnp.where(live, turned[:, :LANES], 0.0)


def finish(rows_live, starts, shifts, counts, pieces, basis):
    rows = pieces.shape[1]
    scalar, vector = pl.BlockSpec(memory_space=pltpu.SMEM), pl.BlockSpec(memory_space=pltpu.VMEM)
    return pl.pallas_call(
        finish_kernel,
        out_shape=jax.ShapeDtypeStruct((rows, basis), jnp.float32),
        in_specs=[scalar] * 4 + [vector],
        out_specs=vector,
        scratch_shapes=[pltpu.VMEM((rows, LIVE), jnp.float32)],
    )(rows_live, starts, shifts, counts, pieces)


def per_device(three_index, density, pair_blocks, basis_counts):
    aux_here, own_blocks, neigh, size, _ = three_index.shape
    rows_here, basis = density.shape
    blocks = basis // size
    x, core = lax.axis_index("x"), lax.axis_index("core")
    zy = lax.axis_index("z") * lax.axis_size("y") + lax.axis_index("y")
    first_row = (x * CORES + core) * own_blocks * size + zy * rows_here

    numbers = jnp.arange(blocks)
    offsets = jnp.sum(jnp.where(numbers[None, :] < numbers[:, None], basis_counts[None, :], 0), axis=1)
    starts = jnp.minimum(offsets // LANES, LIVE // LANES - 2)
    shifts = offsets - starts * LANES

    rows_live = jnp.sum(jnp.where(numbers == first_row // size, basis_counts, 0)) - first_row % size
    column_live = (jnp.arange(size)[None, :] < basis_counts[:, None]).reshape(basis)
    live = (jnp.arange(rows_here) < rows_live)[:, None] & column_live[None, :]

    kept = jnp.where(live, density, 0)
    whole = lax.all_gather(kept, ("x", "core", "z", "y"), axis=0, tiled=True)

    parted = three_index.reshape(SIDE, aux_here // SIDE, own_blocks, neigh, size, size)
    own = lax.all_to_all(parted, "x", 0, 0, tiled=True)
    other = lax.ppermute(own, "core", [(0, 1), (1, 0)])

    partial = exchange_rows(
        core.astype(jnp.int32).reshape(1), pair_blocks.reshape(-1), starts, shifts, basis_counts,
        own, other, whole,
    )
    pieces = lax.all_to_all(partial.reshape(-1, rows_here, LIVE), ("x", "z", "y"), 0, 0, tiled=True)
    return finish(rows_live.astype(jnp.int32).reshape(1), starts, shifts, basis_counts, pieces, basis)


def solution(mesh):
    devices = mesh.devices.reshape(SIDE, CORES, SIDE, SIDE)
    fine = Mesh(devices, ("x", "core", "z", "y"))
    in_specs = (P(("z", "y"), ("x", "core")), P(("x", "core", "z", "y"), None), P(), P())
    out_specs = P(("x", "core", "z", "y"), None)
    return jax.shard_map(
        per_device, mesh=fine, in_specs=in_specs, out_specs=out_specs, check_vma=False
    )
```

```python
import jax
import jax.numpy as jnp
from jax import lax
from jax.experimental import pallas as pl
from jax.experimental.pallas import tpu as pltpu
from jax.sharding import Mesh, PartitionSpec as P

CORES = 2
SIDE = 4
LIVE = 1536
LANES = 128
PIECE = 128


def stacked(tensor, source, mi, aux, neigh):
    return jnp.concatenate(
        [
            jnp.concatenate([tensor[source, p, mi, j] for j in range(neigh)], axis=1)
            for p in range(aux)
        ],
        axis=0,
    )


def halfway_kernel(place, pairs, own, here_a, there_a, here_b, there_b, out_ref, density, sems):
    _, aux, per_source, neigh, size, _ = own.shape
    piece = density.shape[-2]
    half, source = pl.program_id(0), pl.program_id(1)
    x, core, z, y = place[0], place[1], place[2], place[3]

    def copies(here, there, first):
        return [
            pltpu.make_async_copy(here, density.at[first // 2, 0], sems.at[first]),
            pltpu.make_async_copy(there, density.at[first // 2, 1], sems.at[first + 1]),
        ]

    copies_a, copies_b = copies(here_a, there_a, 0), copies(here_b, there_b, 2)

    @pl.when((half == 0) & (source == 0))
    def _():
        for copy in copies_a + copies_b:
            copy.start()
        for copy in copies_a:
            copy.wait()

    @pl.when((half == 1) & (source == 0))
    def _():
        for copy in copies_b:
            copy.wait()

    for mi in range(per_source):
        block = (source * CORES + core) * per_source + mi
        lhs = stacked(own, 0, mi, aux, neigh)
        near = []
        for j in range(neigh):
            partner = pairs[block * neigh + j]
            back_x = lax.rem(x - partner // (CORES * per_source) + SIDE, SIDE)
            swap = jnp.where(partner // per_source % CORES == core, 0, 1)
            for zy in range(size // piece):
                from_z = partner % per_source * (SIDE // per_source) + zy // SIDE
                back_z = lax.rem(z - from_z + SIDE, SIDE)
                back_y = lax.rem(y - zy % SIDE + SIDE, SIDE)
                outer = jnp.where(half == 0, back_y, back_z)
                inner = jnp.where(half == 0, back_z, back_y)
                near.append(density[half, swap, outer, inner, back_x])
        product = jnp.dot(
            lhs, jnp.concatenate(near, axis=0), preferred_element_type=jnp.float32
        ).astype(jnp.bfloat16)
        for k in range(out_ref.shape[0]):
            for p in range(aux):
                out_ref[k, mi * size : (mi + 1) * size, p * size : (p + 1) * size] = product[
                    p * size : (p + 1) * size, k * size : (k + 1) * size
                ]


def halfway_rows(place, pairs, own, here_a, there_a, here_b, there_b):
    sources, aux, per_source, neigh, size, _ = own.shape
    width = here_a.shape[-1]
    blocks = 2 * width // size
    rows = sources * per_source * size
    anywhere = pl.BlockSpec(memory_space=pl.ANY)
    return pl.pallas_call(
        halfway_kernel,
        out_shape=jax.ShapeDtypeStruct((blocks, rows, aux * size), jnp.bfloat16),
        grid_spec=pltpu.PrefetchScalarGridSpec(
            num_scalar_prefetch=2,
            grid=(2, sources),
            in_specs=[
                pl.BlockSpec((1,) + own.shape[1:], lambda h, s, *_: (s, 0, 0, 0, 0, 0)),
            ] + [anywhere] * 4,
            out_specs=pl.BlockSpec(
                (blocks // 2, per_source * size, aux * size), lambda h, s, *_: (h, s, 0)
            ),
            scratch_shapes=[
                pltpu.VMEM((2, CORES) + here_a.shape, jnp.bfloat16),
                pltpu.SemaphoreType.DMA((4,)),
            ],
        ),
        compiler_params=pltpu.CompilerParams(vmem_limit_bytes=36 << 20),
        cost_estimate=pl.CostEstimate(
            flops=2 * rows * aux * neigh * size * 2 * width,
            bytes_accessed=4 * own.size + 8 * here_a.size + 2 * blocks * rows * aux * size,
            transcendentals=0,
        ),
    )(place, pairs, own, here_a, there_a, here_b, there_b)


def exchange_kernel(place, pairs, starts, shifts, counts, own, other, from_own, from_other,
                    out_ref, total):
    _, aux, _, neigh, size, _ = own.shape
    _, rows, _ = from_own.shape
    step = pl.program_id(0)
    per_source = pl.num_programs(0) // SIDE

    @pl.when(step == 0)
    def _():
        total[...] = jnp.zeros_like(total)

    for which, tensor, halfway in ((place[1], own, from_own), (1 - place[1], other, from_other)):
        block = (step // per_source * CORES + which) * per_source + step % per_source
        rhs = stacked(tensor, 0, 0, aux, neigh)
        for r in range(0, rows, PIECE):
            product = jnp.dot(halfway[0, r : r + PIECE], rhs, preferred_element_type=jnp.float32)
            for j in range(neigh):
                total[pairs[block * neigh + j], r : r + PIECE] += product[
                    :, j * size : (j + 1) * size
                ]

    @pl.when(step == pl.num_programs(0) - 1)
    def _():
        out_ref[...] = jnp.zeros_like(out_ref)
        row = lax.broadcasted_iota(jnp.int32, (size, 2 * LANES), 0)
        column = lax.broadcasted_iota(jnp.int32, (size, 2 * LANES), 1)

        def pack(n, carry):
            chosen = (column == row + shifts[n]) & (row < counts[n])
            moved = jnp.dot(
                total[n].astype(jnp.bfloat16),
                jnp.where(chosen, 1.0, 0.0).astype(jnp.bfloat16),
                preferred_element_type=jnp.float32,
            ).astype(jnp.bfloat16)
            at = pl.ds(pl.multiple_of(starts[n] * LANES, LANES), 2 * LANES)
            out_ref[:, at] += moved
            return carry

        lax.fori_loop(0, total.shape[0], pack, 0)


def exchange_rows(place, pairs, starts, shifts, counts, own, other, halfway):
    sources, aux, per_source, neigh, size, _ = own.shape
    blocks, rows, _ = halfway.shape

    def tensor_map(i, *_):
        return (i // per_source, 0, i % per_source, 0, 0, 0)

    def halfway_map(swap):
        def at(i, place, *_):
            which = place[1] if swap == 0 else 1 - place[1]
            return ((i // per_source * CORES + which) * per_source + i % per_source, 0, 0)

        return at

    tensor = pl.BlockSpec((1, aux, 1, neigh, size, size), tensor_map)
    return pl.pallas_call(
        exchange_kernel,
        out_shape=jax.ShapeDtypeStruct((rows, LIVE), jnp.bfloat16),
        grid_spec=pltpu.PrefetchScalarGridSpec(
            num_scalar_prefetch=5,
            grid=(sources * per_source,),
            in_specs=[tensor, tensor] + [
                pl.BlockSpec((1, rows, aux * size), halfway_map(swap)) for swap in range(CORES)
            ],
            out_specs=pl.BlockSpec((rows, LIVE), lambda i, *_: (0, 0)),
            scratch_shapes=[pltpu.VMEM((blocks, rows, size), jnp.float32)],
        ),
        compiler_params=pltpu.CompilerParams(vmem_limit_bytes=36 << 20),
        cost_estimate=pl.CostEstimate(
            flops=2 * rows * aux * neigh * size * blocks * size,
            bytes_accessed=4 * own.size + 2 * halfway.size + 2 * rows * LIVE,
            transcendentals=0,
        ),
    )(place, pairs, starts, shifts, counts, own, other, halfway, halfway)


def finish_kernel(rows_live, starts, shifts, counts, pieces, out_ref, summed):
    amount, rows, _ = pieces.shape
    summed[...] = jnp.zeros_like(summed)

    def add(i, carry):
        part = pieces[pl.ds(i * 8, 8)].astype(jnp.float32)
        summed[...] += jnp.sum(part, axis=0)
        return carry

    lax.fori_loop(0, amount // 8, add, 0)
    row = lax.broadcasted_iota(jnp.int32, (rows, LANES), 0)
    lane = lax.broadcasted_iota(jnp.int32, (rows, LANES), 1)
    for n in range(out_ref.shape[1] // LANES):
        window = summed[:, pl.ds(pl.multiple_of(starts[n] * LANES, LANES), 2 * LANES)]
        turned = pltpu.roll(window, lax.rem(2 * LANES - shifts[n], 2 * LANES), axis=1)
        live = (lane < counts[n]) & (row < rows_live[0])
        out_ref[:, n * LANES : (n + 1) * LANES] = jnp.where(live, turned[:, :LANES], 0.0)


def finish(rows_live, starts, shifts, counts, pieces, basis):
    rows = pieces.shape[1]
    scalar, vector = pl.BlockSpec(memory_space=pltpu.SMEM), pl.BlockSpec(memory_space=pltpu.VMEM)
    return pl.pallas_call(
        finish_kernel,
        out_shape=jax.ShapeDtypeStruct((rows, basis), jnp.float32),
        in_specs=[scalar] * 4 + [vector],
        out_specs=vector,
        scratch_shapes=[pltpu.VMEM((rows, LIVE), jnp.float32)],
    )(rows_live, starts, shifts, counts, pieces)


def moved(value, axis, shift):
    return lax.ppermute(value, axis, [(k, (k + shift) % SIDE) for k in range(SIDE)])


def swapped(value):
    return lax.ppermute(value, "core", [(0, 1), (1, 0)])


def ring(value, axis):
    up, down = moved(value, axis, 1), moved(value, axis, SIDE - 1)
    cut = value.shape[0] // 2
    far = [moved(up[:cut], axis, 1), moved(down[cut:], axis, SIDE - 1)]
    return jnp.stack([value, up, jnp.concatenate(far), down])


def per_device(three_index, density, pair_blocks, basis_counts):
    aux_here, own_blocks, neigh, size, _ = three_index.shape
    rows_here, basis = density.shape
    blocks = basis // size
    x, core, z, y = (lax.axis_index(name) for name in ("x", "core", "z", "y"))
    first_row = (x * CORES + core) * own_blocks * size + (z * SIDE + y) * rows_here

    numbers = jnp.arange(blocks)
    offsets = jnp.sum(jnp.where(numbers[None, :] < numbers[:, None], basis_counts[None, :], 0), axis=1)
    starts = jnp.minimum(offsets // LANES, LIVE // LANES - 2)
    shifts = offsets - starts * LANES

    rows_live = jnp.sum(jnp.where(numbers == first_row // size, basis_counts, 0)) - first_row % size
    column_live = (jnp.arange(size)[None, :] < basis_counts[:, None]).reshape(basis)
    live = (jnp.arange(rows_here) < rows_live)[:, None] & column_live[None, :]

    kept = jnp.where(live, density, 0)
    lines = jnp.stack([kept] + [moved(kept, "x", s) for s in range(1, SIDE)])
    here_a = ring(ring(lines[..., : basis // 2], "z"), "y")
    here_b = ring(ring(lines[..., basis // 2 :], "y"), "z")
    there_a, there_b = swapped(here_a), swapped(here_b)

    parted = three_index.reshape(SIDE, aux_here // SIDE, own_blocks, neigh, size, size)
    own = lax.all_to_all(parted, "x", 0, 0, tiled=True)
    own, there_a, there_b = lax.optimization_barrier((own, there_a, there_b))
    other = swapped(own)

    place = jnp.stack([x, core, z, y]).astype(jnp.int32)
    pairs = pair_blocks.reshape(-1)
    halfway = halfway_rows(place, pairs, own, here_a, there_a, here_b, there_b)
    partial = exchange_rows(place, pairs, starts, shifts, basis_counts, own, other, halfway)
    pieces = lax.all_to_all(partial.reshape(-1, rows_here, LIVE), ("x", "z", "y"), 0, 0, tiled=True)
    return finish(rows_live.astype(jnp.int32).reshape(1), starts, shifts, basis_counts, pieces, basis)


def solution(mesh):
    devices = mesh.devices.reshape(SIDE, CORES, SIDE, SIDE)
    fine = Mesh(devices, ("x", "core", "z", "y"))
    in_specs = (P(("z", "y"), ("x", "core")), P(("x", "core", "z", "y"), None), P(), P())
    out_specs = P(("x", "core", "z", "y"), None)
    return jax.shard_map(
        per_device, mesh=fine, in_specs=in_specs, out_specs=out_specs, check_vma=False
    )
```

```python
import functools

import jax
import jax.numpy as jnp
from jax import lax
from jax.experimental import pallas as pl
from jax.experimental.pallas import tpu as pltpu
from jax.sharding import Mesh, PartitionSpec as P

CORES = 2
SIDE = 4
LIVE = 1536
LANES = 128
PIECE = 128


def stacked(tensor, source, mi, aux, neigh):
    return jnp.concatenate(
        [
            jnp.concatenate([tensor[source, p, mi, j] for j in range(neigh)], axis=1)
            for p in range(aux)
        ],
        axis=0,
    )


def halfway_kernel(y_first, place, pairs, own, here_hbm, there_hbm, out_ref, density, sems):
    _, aux, per_source, neigh, size, _ = own.shape
    piece = density.shape[-2]
    source = pl.program_id(0)
    x, core, z, y = place[0], place[1], place[2], place[3]

    @pl.when(source == 0)
    def _():
        copies = [
            pltpu.make_async_copy(here_hbm, density.at[0], sems.at[0]),
            pltpu.make_async_copy(there_hbm, density.at[1], sems.at[1]),
        ]
        for copy in copies:
            copy.start()
        for copy in copies:
            copy.wait()

    for mi in range(per_source):
        block = (source * CORES + core) * per_source + mi
        lhs = stacked(own, 0, mi, aux, neigh)
        near = []
        for j in range(neigh):
            partner = pairs[block * neigh + j]
            back_x = lax.rem(x - partner // (CORES * per_source) + SIDE, SIDE)
            swap = jnp.where(partner // per_source % CORES == core, 0, 1)
            for zy in range(size // piece):
                from_z = partner % per_source * (SIDE // per_source) + zy // SIDE
                back_z = lax.rem(z - from_z + SIDE, SIDE)
                back_y = lax.rem(y - zy % SIDE + SIDE, SIDE)
                outer, inner = (back_y, back_z) if y_first else (back_z, back_y)
                near.append(density[swap, outer, inner, back_x])
        product = jnp.dot(
            lhs, jnp.concatenate(near, axis=0), preferred_element_type=jnp.float32
        ).astype(jnp.bfloat16)
        for k in range(out_ref.shape[0]):
            for p in range(aux):
                out_ref[k, mi * size : (mi + 1) * size, p * size : (p + 1) * size] = product[
                    p * size : (p + 1) * size, k * size : (k + 1) * size
                ]


def halfway_rows(y_first, place, pairs, own, here, there):
    sources, aux, per_source, neigh, size, _ = own.shape
    width = here.shape[-1]
    blocks = width // size
    rows = sources * per_source * size
    anywhere = pl.BlockSpec(memory_space=pl.ANY)
    return pl.pallas_call(
        functools.partial(halfway_kernel, y_first),
        out_shape=jax.ShapeDtypeStruct((blocks, rows, aux * size), jnp.bfloat16),
        grid_spec=pltpu.PrefetchScalarGridSpec(
            num_scalar_prefetch=2,
            grid=(sources,),
            in_specs=[
                pl.BlockSpec((1,) + own.shape[1:], lambda s, *_: (s, 0, 0, 0, 0, 0)),
                anywhere,
                anywhere,
            ],
            out_specs=pl.BlockSpec((blocks, per_source * size, aux * size), lambda s, *_: (0, s, 0)),
            scratch_shapes=[
                pltpu.VMEM((CORES,) + here.shape, jnp.bfloat16),
                pltpu.SemaphoreType.DMA((CORES,)),
            ],
        ),
        compiler_params=pltpu.CompilerParams(vmem_limit_bytes=20 << 20),
        cost_estimate=pl.CostEstimate(
            flops=2 * rows * aux * neigh * size * width,
            bytes_accessed=2 * own.size + 4 * here.size + 2 * blocks * rows * aux * size,
            transcendentals=0,
        ),
    )(place, pairs, own, here, there)


def exchange_kernel(place, pairs, starts, shifts, counts, own, other, own_a, other_a,
                    own_b, other_b, out_ref, total):
    _, aux, _, neigh, size, _ = own.shape
    _, rows, _ = own_a.shape
    step = pl.program_id(0)
    per_source = pl.num_programs(0) // SIDE

    @pl.when(step == 0)
    def _():
        total[...] = jnp.zeros_like(total)

    def add_in(which, tensor, halfway):
        block = (step // per_source * CORES + which) * per_source + step % per_source
        rhs = stacked(tensor, 0, 0, aux, neigh)
        for r in range(0, rows, PIECE):
            product = jnp.dot(halfway[0, r : r + PIECE], rhs, preferred_element_type=jnp.float32)
            for j in range(neigh):
                total[pairs[block * neigh + j], r : r + PIECE] += product[
                    :, j * size : (j + 1) * size
                ]

    @pl.when(step < pl.num_programs(0) // 2)
    def _():
        add_in(place[1], own, own_a)
        add_in(1 - place[1], other, other_a)

    @pl.when(step >= pl.num_programs(0) // 2)
    def _():
        add_in(place[1], own, own_b)
        add_in(1 - place[1], other, other_b)

    @pl.when(step == pl.num_programs(0) - 1)
    def _():
        out_ref[...] = jnp.zeros_like(out_ref)
        row = lax.broadcasted_iota(jnp.int32, (size, 2 * LANES), 0)
        column = lax.broadcasted_iota(jnp.int32, (size, 2 * LANES), 1)

        def pack(n, carry):
            chosen = (column == row + shifts[n]) & (row < counts[n])
            moved = jnp.dot(
                total[n].astype(jnp.bfloat16),
                jnp.where(chosen, 1.0, 0.0).astype(jnp.bfloat16),
                preferred_element_type=jnp.float32,
            ).astype(jnp.bfloat16)
            at = pl.ds(pl.multiple_of(starts[n] * LANES, LANES), 2 * LANES)
            out_ref[:, at] += moved
            return carry

        lax.fori_loop(0, total.shape[0], pack, 0)


def exchange_rows(place, pairs, starts, shifts, counts, own, other, halfway_a, halfway_b):
    sources, aux, per_source, neigh, size, _ = own.shape
    half, rows, _ = halfway_a.shape
    blocks = 2 * half

    def tensor_map(i, *_):
        return (i // per_source, 0, i % per_source, 0, 0, 0)

    def halfway_map(swap, first):
        def at(i, place, *_):
            which = place[1] if swap == 0 else 1 - place[1]
            block = (i // per_source * CORES + which) * per_source + i % per_source - first
            return (jnp.clip(block, 0, half - 1), 0, 0)

        return at

    tensor = pl.BlockSpec((1, aux, 1, neigh, size, size), tensor_map)
    return pl.pallas_call(
        exchange_kernel,
        out_shape=jax.ShapeDtypeStruct((rows, LIVE), jnp.bfloat16),
        grid_spec=pltpu.PrefetchScalarGridSpec(
            num_scalar_prefetch=5,
            grid=(sources * per_source,),
            in_specs=[tensor, tensor] + [
                pl.BlockSpec((1, rows, aux * size), halfway_map(swap, first))
                for first in (0, half)
                for swap in range(CORES)
            ],
            out_specs=pl.BlockSpec((rows, LIVE), lambda i, *_: (0, 0)),
            scratch_shapes=[pltpu.VMEM((blocks, rows, size), jnp.float32)],
        ),
        compiler_params=pltpu.CompilerParams(vmem_limit_bytes=32 << 20),
        cost_estimate=pl.CostEstimate(
            flops=2 * rows * aux * neigh * size * blocks * size,
            bytes_accessed=4 * own.size + 4 * halfway_a.size + 2 * rows * LIVE,
            transcendentals=0,
        ),
    )(place, pairs, starts, shifts, counts, own, other, halfway_a, halfway_a, halfway_b, halfway_b)


def finish_kernel(rows_live, starts, shifts, counts, pieces, out_ref, summed):
    amount, rows, _ = pieces.shape
    summed[...] = jnp.zeros_like(summed)

    def add(i, carry):
        part = pieces[pl.ds(i * 8, 8)].astype(jnp.float32)
        summed[...] += jnp.sum(part, axis=0)
        return carry

    lax.fori_loop(0, amount // 8, add, 0)
    row = lax.broadcasted_iota(jnp.int32, (rows, LANES), 0)
    lane = lax.broadcasted_iota(jnp.int32, (rows, LANES), 1)
    for n in range(out_ref.shape[1] // LANES):
        window = summed[:, pl.ds(pl.multiple_of(starts[n] * LANES, LANES), 2 * LANES)]
        turned = pltpu.roll(window, lax.rem(2 * LANES - shifts[n], 2 * LANES), axis=1)
        live = (lane < counts[n]) & (row < rows_live[0])
        out_ref[:, n * LANES : (n + 1) * LANES] = jnp.where(live, turned[:, :LANES], 0.0)


def finish(rows_live, starts, shifts, counts, pieces, basis):
    rows = pieces.shape[1]
    scalar, vector = pl.BlockSpec(memory_space=pltpu.SMEM), pl.BlockSpec(memory_space=pltpu.VMEM)
    return pl.pallas_call(
        finish_kernel,
        out_shape=jax.ShapeDtypeStruct((rows, basis), jnp.float32),
        in_specs=[scalar] * 4 + [vector],
        out_specs=vector,
        scratch_shapes=[pltpu.VMEM((rows, LIVE), jnp.float32)],
    )(rows_live, starts, shifts, counts, pieces)


def moved(value, axis, shift):
    return lax.ppermute(value, axis, [(k, (k + shift) % SIDE) for k in range(SIDE)])


def swapped(value):
    return lax.ppermute(value, "core", [(0, 1), (1, 0)])


def ring(value, axis):
    up, down = moved(value, axis, 1), moved(value, axis, SIDE - 1)
    cut = value.shape[0] // 2
    far = [moved(up[:cut], axis, 1), moved(down[cut:], axis, SIDE - 1)]
    return jnp.stack([value, up, jnp.concatenate(far), down])


def per_device(three_index, density, pair_blocks, basis_counts):
    aux_here, own_blocks, neigh, size, _ = three_index.shape
    rows_here, basis = density.shape
    blocks = basis // size
    x, core, z, y = (lax.axis_index(name) for name in ("x", "core", "z", "y"))
    first_row = (x * CORES + core) * own_blocks * size + (z * SIDE + y) * rows_here

    numbers = jnp.arange(blocks)
    offsets = jnp.sum(jnp.where(numbers[None, :] < numbers[:, None], basis_counts[None, :], 0), axis=1)
    starts = jnp.minimum(offsets // LANES, LIVE // LANES - 2)
    shifts = offsets - starts * LANES

    rows_live = jnp.sum(jnp.where(numbers == first_row // size, basis_counts, 0)) - first_row % size
    column_live = (jnp.arange(size)[None, :] < basis_counts[:, None]).reshape(basis)
    live = (jnp.arange(rows_here) < rows_live)[:, None] & column_live[None, :]

    kept = jnp.where(live, density, 0)
    lines = jnp.stack([kept] + [moved(kept, "x", s) for s in range(1, SIDE)])
    lines, three_index = lax.optimization_barrier((lines, three_index))
    here_a = ring(ring(lines[..., : basis // 2], "z"), "y")
    here_b = ring(ring(lines[..., basis // 2 :], "y"), "z")

    parted = three_index.reshape(SIDE, aux_here // SIDE, own_blocks, neigh, size, size)
    own = lax.all_to_all(parted, "x", 0, 0, tiled=True)
    own, here_a, here_b = lax.optimization_barrier((own, here_a, here_b))
    there_a = swapped(here_a)
    there_a, here_b = lax.optimization_barrier((there_a, here_b))
    there_b = swapped(here_b)

    place = jnp.stack([x, core, z, y]).astype(jnp.int32)
    pairs = pair_blocks.reshape(-1)
    halfway_a = halfway_rows(True, place, pairs, own, here_a, there_a)
    halfway_a, there_b, sent = lax.optimization_barrier((halfway_a, there_b, own))
    other = swapped(sent)
    halfway_b = halfway_rows(False, place, pairs, own, here_b, there_b)
    partial = exchange_rows(
        place, pairs, starts, shifts, basis_counts, own, other, halfway_a, halfway_b
    )
    pieces = lax.all_to_all(partial.reshape(-1, rows_here, LIVE), ("x", "z", "y"), 0, 0, tiled=True)
    return finish(rows_live.astype(jnp.int32).reshape(1), starts, shifts, basis_counts, pieces, basis)


def solution(mesh):
    devices = mesh.devices.reshape(SIDE, CORES, SIDE, SIDE)
    fine = Mesh(devices, ("x", "core", "z", "y"))
    in_specs = (P(("z", "y"), ("x", "core")), P(("x", "core", "z", "y"), None), P(), P())
    out_specs = P(("x", "core", "z", "y"), None)
    return jax.shard_map(
        per_device, mesh=fine, in_specs=in_specs, out_specs=out_specs, check_vma=False
    )
```

```python
import functools

import jax
import jax.numpy as jnp
from jax import lax
from jax.experimental import pallas as pl
from jax.experimental.pallas import tpu as pltpu
from jax.sharding import Mesh, PartitionSpec as P

CORES = 2
SIDE = 4
LIVE = 1536
LANES = 128
PIECE = 128
PARTS = 2


def stacked(tensor, source, mi, aux, neigh):
    return jnp.concatenate(
        [
            jnp.concatenate([tensor[source, p, mi, j] for j in range(neigh)], axis=1)
            for p in range(aux)
        ],
        axis=0,
    )


def halfway_kernel(y_first, place, pairs, own, here_hbm, there_hbm, out_ref, density, sems):
    _, aux, per_source, neigh, size, _ = own.shape
    piece = density.shape[-2]
    source = pl.program_id(0)
    x, core, z, y = place[0], place[1], place[2], place[3]

    @pl.when(source == 0)
    def _():
        copies = [
            pltpu.make_async_copy(here_hbm, density.at[0], sems.at[0]),
            pltpu.make_async_copy(there_hbm, density.at[1], sems.at[1]),
        ]
        for copy in copies:
            copy.start()
        for copy in copies:
            copy.wait()

    for mi in range(per_source):
        block = (source * CORES + core) * per_source + mi
        lhs = stacked(own, 0, mi, aux, neigh)
        near = []
        for j in range(neigh):
            partner = pairs[block * neigh + j]
            back_x = lax.rem(x - partner // (CORES * per_source) + SIDE, SIDE)
            swap = jnp.where(partner // per_source % CORES == core, 0, 1)
            for zy in range(size // piece):
                from_z = partner % per_source * (SIDE // per_source) + zy // SIDE
                back_z = lax.rem(z - from_z + SIDE, SIDE)
                back_y = lax.rem(y - zy % SIDE + SIDE, SIDE)
                outer, inner = (back_y, back_z) if y_first else (back_z, back_y)
                near.append(density[swap, outer, inner, back_x])
        product = jnp.dot(
            lhs, jnp.concatenate(near, axis=0), preferred_element_type=jnp.float32
        )
        part = piece // PARTS
        rows = size // PARTS
        for p in range(aux):
            for h in range(PARTS):
                chosen = [
                    product[at : at + part]
                    for at in range(p * size + h * part, (p + 1) * size, piece)
                ]
                chosen = jnp.concatenate(chosen, axis=0).astype(jnp.bfloat16)
                for k in range(out_ref.shape[0]):
                    out_ref[k, h, mi * rows : (mi + 1) * rows, p * size : (p + 1) * size] = chosen[
                        :, k * size : (k + 1) * size
                    ]


def halfway_rows(y_first, place, pairs, own, here, there):
    sources, aux, per_source, neigh, size, _ = own.shape
    width = here.shape[-1]
    blocks = width // size
    rows = sources * per_source * size
    anywhere = pl.BlockSpec(memory_space=pl.ANY)
    return pl.pallas_call(
        functools.partial(halfway_kernel, y_first),
        out_shape=jax.ShapeDtypeStruct((blocks, PARTS, rows // PARTS, aux * size), jnp.bfloat16),
        grid_spec=pltpu.PrefetchScalarGridSpec(
            num_scalar_prefetch=2,
            grid=(sources,),
            in_specs=[
                pl.BlockSpec((1,) + own.shape[1:], lambda s, *_: (s, 0, 0, 0, 0, 0)),
                anywhere,
                anywhere,
            ],
            out_specs=pl.BlockSpec(
                (blocks, PARTS, rows // sources // PARTS, aux * size), lambda s, *_: (0, 0, s, 0)
            ),
            scratch_shapes=[
                pltpu.VMEM((CORES,) + here.shape, jnp.bfloat16),
                pltpu.SemaphoreType.DMA((CORES,)),
            ],
        ),
        compiler_params=pltpu.CompilerParams(vmem_limit_bytes=56 << 20),
        cost_estimate=pl.CostEstimate(
            flops=2 * rows * aux * neigh * size * width,
            bytes_accessed=2 * own.size + 4 * here.size + 2 * blocks * rows * aux * size,
            transcendentals=0,
        ),
    )(place, pairs, own, here, there)


def exchange_kernel(place, pairs, starts, shifts, counts, own, other, own_a, other_a,
                    own_b, other_b, out_ref, total):
    _, aux, _, neigh, size, _ = own.shape
    _, _, rows, _ = own_a.shape
    step = pl.program_id(0)
    per_source = pl.num_programs(0) // SIDE

    @pl.when(step == 0)
    def _():
        total[...] = jnp.zeros_like(total)

    def add_in(which, tensor, halfway):
        block = (step // per_source * CORES + which) * per_source + step % per_source
        rhs = stacked(tensor, 0, 0, aux, neigh)
        for r in range(0, rows, PIECE):
            product = jnp.dot(halfway[0, 0, r : r + PIECE], rhs, preferred_element_type=jnp.float32)
            for j in range(neigh):
                total[pairs[block * neigh + j], r : r + PIECE] += product[
                    :, j * size : (j + 1) * size
                ]

    @pl.when(step < pl.num_programs(0) // 2)
    def _():
        add_in(place[1], own, own_a)
        add_in(1 - place[1], other, other_a)

    @pl.when(step >= pl.num_programs(0) // 2)
    def _():
        add_in(place[1], own, own_b)
        add_in(1 - place[1], other, other_b)

    @pl.when(step == pl.num_programs(0) - 1)
    def _():
        out_ref[...] = jnp.zeros_like(out_ref)
        row = lax.broadcasted_iota(jnp.int32, (size, 2 * LANES), 0)
        column = lax.broadcasted_iota(jnp.int32, (size, 2 * LANES), 1)

        def pack(n, carry):
            chosen = (column == row + shifts[n]) & (row < counts[n])
            moved = jnp.dot(
                total[n].astype(jnp.bfloat16),
                jnp.where(chosen, 1.0, 0.0).astype(jnp.bfloat16),
                preferred_element_type=jnp.float32,
            ).astype(jnp.bfloat16)
            at = pl.ds(pl.multiple_of(starts[n] * LANES, LANES), 2 * LANES)
            out_ref[:, at] += moved
            return carry

        lax.fori_loop(0, total.shape[0], pack, 0)


def exchange_rows(part, place, pairs, starts, shifts, counts, own, other, halfway_a, halfway_b):
    sources, aux, per_source, neigh, size, _ = own.shape
    half, _, rows, _ = halfway_a.shape
    blocks = 2 * half

    def tensor_map(i, *_):
        return (i // per_source, 0, i % per_source, 0, 0, 0)

    def halfway_map(swap, first):
        def at(i, place, *_):
            which = place[1] if swap == 0 else 1 - place[1]
            block = (i // per_source * CORES + which) * per_source + i % per_source - first
            return (jnp.clip(block, 0, half - 1), part, 0, 0)

        return at

    tensor = pl.BlockSpec((1, aux, 1, neigh, size, size), tensor_map)
    return pl.pallas_call(
        exchange_kernel,
        out_shape=jax.ShapeDtypeStruct((rows, LIVE), jnp.bfloat16),
        grid_spec=pltpu.PrefetchScalarGridSpec(
            num_scalar_prefetch=5,
            grid=(sources * per_source,),
            in_specs=[tensor, tensor] + [
                pl.BlockSpec((1, 1, rows, aux * size), halfway_map(swap, first))
                for first in (0, half)
                for swap in range(CORES)
            ],
            out_specs=pl.BlockSpec((rows, LIVE), lambda i, *_: (0, 0)),
            scratch_shapes=[pltpu.VMEM((blocks, rows, size), jnp.float32)],
        ),
        compiler_params=pltpu.CompilerParams(vmem_limit_bytes=56 << 20),
        cost_estimate=pl.CostEstimate(
            flops=2 * rows * aux * neigh * size * blocks * size,
            bytes_accessed=4 * own.size + 2 * halfway_a.size + 2 * rows * LIVE,
            transcendentals=0,
        ),
    )(place, pairs, starts, shifts, counts, own, other, halfway_a, halfway_a, halfway_b, halfway_b)


def finish_kernel(rows_live, starts, shifts, counts, pieces, out_ref, summed):
    amount, rows, _ = pieces.shape
    summed[...] = jnp.zeros_like(summed)

    def add(i, carry):
        part = pieces[pl.ds(i * 8, 8)].astype(jnp.float32)
        summed[...] += jnp.sum(part, axis=0)
        return carry

    lax.fori_loop(0, amount // 8, add, 0)
    row = lax.broadcasted_iota(jnp.int32, (rows, LANES), 0)
    lane = lax.broadcasted_iota(jnp.int32, (rows, LANES), 1)
    for n in range(out_ref.shape[1] // LANES):
        window = summed[:, pl.ds(pl.multiple_of(starts[n] * LANES, LANES), 2 * LANES)]
        turned = pltpu.roll(window, lax.rem(2 * LANES - shifts[n], 2 * LANES), axis=1)
        live = (lane < counts[n]) & (row < rows_live[0])
        out_ref[:, n * LANES : (n + 1) * LANES] = jnp.where(live, turned[:, :LANES], 0.0)


def finish(rows_live, starts, shifts, counts, pieces, basis):
    rows = pieces.shape[1]
    scalar, vector = pl.BlockSpec(memory_space=pltpu.SMEM), pl.BlockSpec(memory_space=pltpu.VMEM)
    return pl.pallas_call(
        finish_kernel,
        out_shape=jax.ShapeDtypeStruct((rows, basis), jnp.float32),
        in_specs=[scalar] * 4 + [vector],
        out_specs=vector,
        scratch_shapes=[pltpu.VMEM((rows, LIVE), jnp.float32)],
    )(rows_live, starts, shifts, counts, pieces)


def moved(value, axis, shift):
    return lax.ppermute(value, axis, [(k, (k + shift) % SIDE) for k in range(SIDE)])


def swapped(value):
    return lax.ppermute(value, "core", [(0, 1), (1, 0)])


def ring(value, axis):
    up, down = moved(value, axis, 1), moved(value, axis, SIDE - 1)
    cut = value.shape[0] // 2
    far = [moved(up[:cut], axis, 1), moved(down[cut:], axis, SIDE - 1)]
    return jnp.stack([value, up, jnp.concatenate(far), down])


def per_device(three_index, density, pair_blocks, basis_counts):
    aux_here, own_blocks, neigh, size, _ = three_index.shape
    rows_here, basis = density.shape
    blocks = basis // size
    x, core, z, y = (lax.axis_index(name) for name in ("x", "core", "z", "y"))

    numbers = jnp.arange(blocks)
    offsets = jnp.sum(jnp.where(numbers[None, :] < numbers[:, None], basis_counts[None, :], 0), axis=1)
    starts = jnp.minimum(offsets // LANES, LIVE // LANES - 2)
    shifts = offsets - starts * LANES

    from_x = lax.rem(x - jnp.arange(SIDE) + SIDE, SIDE)
    first_row = (from_x * CORES + core) * own_blocks * size + (z * SIDE + y) * rows_here
    chosen = numbers[None, :] == (first_row // size)[:, None]
    rows_live = jnp.sum(jnp.where(chosen, basis_counts[None, :], 0), axis=1) - first_row % size
    column_live = (jnp.arange(size)[None, :] < basis_counts[:, None]).reshape(basis)
    live = (jnp.arange(rows_here)[None, :] < rows_live[:, None])[:, :, None] & column_live

    lines = jnp.stack([density] + [moved(density, "x", s) for s in range(1, SIDE)])
    lines = jnp.where(live, lines, 0)
    lines, three_index = lax.optimization_barrier((lines, three_index))
    here_a = ring(ring(lines[..., : basis // 2], "z"), "y")
    here_b = ring(ring(lines[..., basis // 2 :], "y"), "z")

    parted = three_index.reshape(SIDE, aux_here // SIDE, own_blocks, neigh, size, size)
    own = lax.all_to_all(parted, "x", 0, 0, tiled=True)
    own, here_a, here_b = lax.optimization_barrier((own, here_a, here_b))
    there_a = swapped(here_a)
    there_a, here_b = lax.optimization_barrier((there_a, here_b))
    there_b = swapped(here_b)

    place = jnp.stack([x, core, z, y]).astype(jnp.int32)
    pairs = pair_blocks.reshape(-1)
    halfway_a = halfway_rows(True, place, pairs, own, here_a, there_a)
    halfway_a, there_b, sent = lax.optimization_barrier((halfway_a, there_b, own))
    other = swapped(sent)
    halfway_b = halfway_rows(False, place, pairs, own, here_b, there_b)
    part_rows = rows_here // PARTS
    outputs = []
    for part in range(PARTS):
        partial = exchange_rows(
            part, place, pairs, starts, shifts, basis_counts, own, other, halfway_a, halfway_b
        )
        partial = partial.reshape(-1, part_rows, LIVE)
        pieces = lax.all_to_all(partial, ("x", "z", "y"), 0, 0, tiled=True)
        still = (rows_live[0] - part * part_rows).astype(jnp.int32).reshape(1)
        outputs.append(finish(still, starts, shifts, basis_counts, pieces, basis))
    return jnp.concatenate(outputs, axis=0)


def solution(mesh):
    devices = mesh.devices.reshape(SIDE, CORES, SIDE, SIDE)
    fine = Mesh(devices, ("x", "core", "z", "y"))
    in_specs = (P(("z", "y"), ("x", "core")), P(("x", "core", "z", "y"), None), P(), P())
    out_specs = P(("x", "core", "z", "y"), None)
    return jax.shard_map(
        per_device, mesh=fine, in_specs=in_specs, out_specs=out_specs, check_vma=False
    )
```

```python
import functools

import jax
import jax.numpy as jnp
from jax import lax
from jax.experimental import pallas as pl
from jax.experimental.pallas import tpu as pltpu
from jax.sharding import Mesh, PartitionSpec as P

CORES = 2
SIDE = 4
LIVE = 1536
LANES = 128
PIECE = 128
PARTS = 2


def stacked(tensor, source, mi, aux, neigh):
    return jnp.concatenate(
        [
            jnp.concatenate([tensor[source, p, mi, j] for j in range(neigh)], axis=1)
            for p in range(aux)
        ],
        axis=0,
    )


def half_stack(tensor, source, mi, aux, neigh, size, part, piece):
    rows = piece // PARTS
    lines = []
    for p in range(aux):
        blocks = []
        for j in range(neigh):
            block = tensor[source, p, mi, j].astype(jnp.float32)
            chosen = [block[at : at + rows] for at in range(part * rows, size, piece)]
            blocks.append(jnp.concatenate(chosen, axis=0).astype(jnp.bfloat16))
        lines.append(jnp.concatenate(blocks, axis=1))
    return jnp.concatenate(lines, axis=0)


def exchange_kernel(part, place, pairs, starts, shifts, counts, own_hbm, other_hbm, here_a, there_a,
                    here_b, there_b, out_ref, own, other, density, halfway, total, sems):
    sources, aux, per_source, neigh, size, _ = own.shape
    piece, width = density.shape[-2:]
    blocks, rows, _ = halfway.shape
    x, core, z, y = place[0], place[1], place[2], place[3]
    part_size = size // PARTS

    def copy(source, target, index):
        return pltpu.make_async_copy(source, target, sems.at[index])

    own_copies = [copy(own_hbm.at[s], own.at[s], s) for s in range(sources)]
    first_copies = [
        copy(here_a, density.at[0, 0], sources),
        copy(there_a, density.at[0, 1], sources + 1),
    ]
    next_copies = [
        copy(here_b, density.at[1, 0], sources + 2),
        copy(there_b, density.at[1, 1], sources + 3),
    ]
    last_copy = copy(other_hbm, other, sources + 4)
    for one in own_copies[:1] + first_copies:
        one.start()
    for one in first_copies:
        one.wait()
    for one in own_copies[1:] + next_copies:
        one.start()
    last_copy.start()

    for half in range(2):
        if half == 1:
            for one in next_copies:
                one.wait()

        def first(b, carry):
            source, mi = b // per_source, b % per_source
            block = (source * CORES + core) * per_source + mi
            lhs = half_stack(own, source, mi, aux, neigh, size, part, piece)
            near = []
            for j in range(neigh):
                partner = pairs[block * neigh + j]
                back_x = lax.rem(x - partner // (CORES * per_source) + SIDE, SIDE)
                swap = jnp.where(partner // per_source % CORES == core, 0, 1)
                for zy in range(size // piece):
                    from_z = partner % per_source * (SIDE // per_source) + zy // SIDE
                    back_z = lax.rem(z - from_z + SIDE, SIDE)
                    back_y = lax.rem(y - zy % SIDE + SIDE, SIDE)
                    outer, inner = (back_y, back_z) if half == 0 else (back_z, back_y)
                    near.append(density[half, swap, outer, inner, back_x])
            product = jnp.dot(
                lhs, jnp.concatenate(near, axis=0), preferred_element_type=jnp.float32
            ).astype(jnp.bfloat16)
            at = pl.ds(pl.multiple_of(b * part_size, part_size), part_size)
            for k in range(width // size):
                for p in range(aux):
                    halfway[half * (width // size) + k, at, p * size : (p + 1) * size] = product[
                        p * part_size : (p + 1) * part_size, k * size : (k + 1) * size
                    ]
            return carry

        for source in range(sources):
            if half == 0:
                own_copies[source].wait()
            lax.fori_loop(source * per_source, (source + 1) * per_source, first, 0, unroll=True)

    total[...] = jnp.zeros_like(total)
    last_copy.wait()

    def add_in(tensor, which):
        def second(b, carry):
            block = (b // per_source * CORES + which) * per_source + b % per_source
            rhs = stacked(tensor, b // per_source, b % per_source, aux, neigh)
            for r in range(0, rows, PIECE):
                product = jnp.dot(
                    halfway[block, r : r + PIECE], rhs, preferred_element_type=jnp.float32
                )
                for j in range(neigh):
                    total[pairs[block * neigh + j], r : r + PIECE] += product[
                        :, j * size : (j + 1) * size
                    ]
            return carry

        lax.fori_loop(0, sources * per_source, second, 0, unroll=4)

    add_in(own, core)
    add_in(other, 1 - core)

    out_ref[...] = jnp.zeros_like(out_ref)
    row = lax.broadcasted_iota(jnp.int32, (size, 2 * LANES), 0)
    column = lax.broadcasted_iota(jnp.int32, (size, 2 * LANES), 1)
    for n in range(blocks):
        chosen = (column == row + shifts[n]) & (row < counts[n])
        moved_columns = jnp.dot(
            total[n].astype(jnp.bfloat16),
            jnp.where(chosen, 1.0, 0.0).astype(jnp.bfloat16),
            preferred_element_type=jnp.float32,
        ).astype(jnp.bfloat16)
        at = pl.ds(pl.multiple_of(starts[n] * LANES, LANES), 2 * LANES)
        out_ref[:, at] += moved_columns


def exchange_rows(part, place, pairs, starts, shifts, counts, own, other, here_a, there_a, here_b, there_b):
    sources, aux, per_source, neigh, size, _ = own.shape
    width = here_a.shape[-1]
    blocks = 2 * width // size
    rows = sources * per_source * size // PARTS
    scalar, vector = pl.BlockSpec(memory_space=pltpu.SMEM), pl.BlockSpec(memory_space=pltpu.VMEM)
    return pl.pallas_call(
        functools.partial(exchange_kernel, part),
        out_shape=jax.ShapeDtypeStruct((rows, LIVE), jnp.bfloat16),
        in_specs=[scalar] * 5 + [pl.BlockSpec(memory_space=pl.ANY)] * 6,
        out_specs=vector,
        scratch_shapes=[
            pltpu.VMEM(own.shape, jnp.bfloat16),
            pltpu.VMEM(own.shape, jnp.bfloat16),
            pltpu.VMEM((2, CORES) + here_a.shape, jnp.bfloat16),
            pltpu.VMEM((blocks, rows, aux * size), jnp.bfloat16),
            pltpu.VMEM((blocks, rows, size), jnp.float32),
            pltpu.SemaphoreType.DMA((sources + 5,)),
        ],
        compiler_params=pltpu.CompilerParams(vmem_limit_bytes=56 << 20),
        cost_estimate=pl.CostEstimate(
            flops=4 * rows * aux * neigh * size * blocks * size,
            bytes_accessed=4 * own.size + 8 * here_a.size + 2 * rows * LIVE,
            transcendentals=0,
        ),
    )(place, pairs, starts, shifts, counts, own, other, here_a, there_a, here_b, there_b)


def finish_kernel(rows_live, starts, shifts, counts, pieces, out_ref, summed):
    amount, rows, _ = pieces.shape
    summed[...] = jnp.zeros_like(summed)

    def add(i, carry):
        part = pieces[pl.ds(i * 8, 8)].astype(jnp.float32)
        summed[...] += jnp.sum(part, axis=0)
        return carry

    lax.fori_loop(0, amount // 8, add, 0)
    row = lax.broadcasted_iota(jnp.int32, (rows, LANES), 0)
    lane = lax.broadcasted_iota(jnp.int32, (rows, LANES), 1)
    for n in range(out_ref.shape[1] // LANES):
        window = summed[:, pl.ds(pl.multiple_of(starts[n] * LANES, LANES), 2 * LANES)]
        turned = pltpu.roll(window, lax.rem(2 * LANES - shifts[n], 2 * LANES), axis=1)
        live = (lane < counts[n]) & (row < rows_live[0])
        out_ref[:, n * LANES : (n + 1) * LANES] = jnp.where(live, turned[:, :LANES], 0.0)


def finish(rows_live, starts, shifts, counts, pieces, basis):
    rows = pieces.shape[1]
    scalar, vector = pl.BlockSpec(memory_space=pltpu.SMEM), pl.BlockSpec(memory_space=pltpu.VMEM)
    return pl.pallas_call(
        finish_kernel,
        out_shape=jax.ShapeDtypeStruct((rows, basis), jnp.float32),
        in_specs=[scalar] * 4 + [vector],
        out_specs=vector,
        scratch_shapes=[pltpu.VMEM((rows, LIVE), jnp.float32)],
    )(rows_live, starts, shifts, counts, pieces)


def moved(value, axis, shift):
    return lax.ppermute(value, axis, [(k, (k + shift) % SIDE) for k in range(SIDE)])


def swapped(value):
    return lax.ppermute(value, "core", [(0, 1), (1, 0)])


def ring(value, axis):
    up, down = moved(value, axis, 1), moved(value, axis, SIDE - 1)
    cut = value.shape[0] // 2
    far = [moved(up[:cut], axis, 1), moved(down[cut:], axis, SIDE - 1)]
    return jnp.stack([value, up, jnp.concatenate(far), down])


def per_device(three_index, density, pair_blocks, basis_counts):
    aux_here, own_blocks, neigh, size, _ = three_index.shape
    rows_here, basis = density.shape
    blocks = basis // size
    x, core, z, y = (lax.axis_index(name) for name in ("x", "core", "z", "y"))

    numbers = jnp.arange(blocks)
    offsets = jnp.sum(jnp.where(numbers[None, :] < numbers[:, None], basis_counts[None, :], 0), axis=1)
    starts = jnp.minimum(offsets // LANES, LIVE // LANES - 2)
    shifts = offsets - starts * LANES

    from_x = lax.rem(x - jnp.arange(SIDE) + SIDE, SIDE)
    first_row = (from_x * CORES + core) * own_blocks * size + (z * SIDE + y) * rows_here
    chosen = numbers[None, :] == (first_row // size)[:, None]
    rows_live = jnp.sum(jnp.where(chosen, basis_counts[None, :], 0), axis=1) - first_row % size
    column_live = (jnp.arange(size)[None, :] < basis_counts[:, None]).reshape(basis)
    live = (jnp.arange(rows_here)[None, :] < rows_live[:, None])[:, :, None] & column_live

    lines = jnp.stack([density] + [moved(density, "x", s) for s in range(1, SIDE)])
    lines = jnp.where(live, lines, 0)
    lines, three_index = lax.optimization_barrier((lines, three_index))
    here_a = ring(ring(lines[..., : basis // 2], "z"), "y")
    here_b = ring(ring(lines[..., basis // 2 :], "y"), "z")

    parted = three_index.reshape(SIDE, aux_here // SIDE, own_blocks, neigh, size, size)
    own = lax.all_to_all(parted, "x", 0, 0, tiled=True)
    own, here_a, here_b = lax.optimization_barrier((own, here_a, here_b))
    there_a, there_b, other = swapped(here_a), swapped(here_b), swapped(own)

    place = jnp.stack([x, core, z, y]).astype(jnp.int32)
    pairs = pair_blocks.reshape(-1)
    part_rows = rows_here // PARTS
    outputs = []
    for part in range(PARTS):
        partial = exchange_rows(
            part, place, pairs, starts, shifts, basis_counts, own, other,
            here_a, there_a, here_b, there_b,
        )
        partial = partial.reshape(-1, part_rows, LIVE)
        pieces = lax.all_to_all(partial, ("x", "z", "y"), 0, 0, tiled=True)
        still = (rows_live[0] - part * part_rows).astype(jnp.int32).reshape(1)
        outputs.append(finish(still, starts, shifts, basis_counts, pieces, basis))
    return jnp.concatenate(outputs, axis=0)


def solution(mesh):
    devices = mesh.devices.reshape(SIDE, CORES, SIDE, SIDE)
    fine = Mesh(devices, ("x", "core", "z", "y"))
    in_specs = (P(("z", "y"), ("x", "core")), P(("x", "core", "z", "y"), None), P(), P())
    out_specs = P(("x", "core", "z", "y"), None)
    return jax.shard_map(
        per_device, mesh=fine, in_specs=in_specs, out_specs=out_specs, check_vma=False
    )
```

```python
import jax
import jax.numpy as jnp
from jax import lax
from jax.experimental import pallas as pl
from jax.experimental.pallas import tpu as pltpu
from jax.sharding import Mesh, PartitionSpec as P

CORES = 2
SIDE = 4
LIVE = 1536
LANES = 128
PIECE = 128


def stacked(tensor, source, mi, aux, neigh):
    return jnp.concatenate(
        [
            jnp.concatenate([tensor[source, p, mi, j] for j in range(neigh)], axis=1)
            for p in range(aux)
        ],
        axis=0,
    )


def exchange_kernel(place, pairs, starts, shifts, counts, own_hbm, other_hbm, here_a, there_a,
                    here_b, there_b, out_ref, own, other, density, halfway, total, sems):
    sources, aux, per_source, neigh, size, _ = own.shape
    piece, width = density.shape[-2:]
    blocks, rows, _ = halfway.shape
    x, core, z, y = place[0], place[1], place[2], place[3]

    def copy(source, target, index):
        return pltpu.make_async_copy(source, target, sems.at[index])

    own_copies = [copy(own_hbm.at[s], own.at[s], s) for s in range(sources)]
    first_copies = [
        copy(here_a, density.at[0, 0], sources),
        copy(there_a, density.at[0, 1], sources + 1),
    ]
    next_copies = [
        copy(here_b, density.at[1, 0], sources + 2),
        copy(there_b, density.at[1, 1], sources + 3),
    ]
    last_copy = copy(other_hbm, other, sources + 4)
    for one in own_copies[:1] + first_copies:
        one.start()
    for one in first_copies:
        one.wait()
    for one in own_copies[1:] + next_copies:
        one.start()
    last_copy.start()

    for half in range(2):
        if half == 1:
            for one in next_copies:
                one.wait()

        def first(b, carry):
            source, mi = b // per_source, b % per_source
            block = (source * CORES + core) * per_source + mi
            lhs = stacked(own, source, mi, aux, neigh)
            near = []
            for j in range(neigh):
                partner = pairs[block * neigh + j]
                back_x = lax.rem(x - partner // (CORES * per_source) + SIDE, SIDE)
                swap = jnp.where(partner // per_source % CORES == core, 0, 1)
                for zy in range(size // piece):
                    from_z = partner % per_source * (SIDE // per_source) + zy // SIDE
                    back_z = lax.rem(z - from_z + SIDE, SIDE)
                    back_y = lax.rem(y - zy % SIDE + SIDE, SIDE)
                    outer, inner = (back_y, back_z) if half == 0 else (back_z, back_y)
                    near.append(density[half, swap, outer, inner, back_x])
            product = jnp.dot(
                lhs, jnp.concatenate(near, axis=0), preferred_element_type=jnp.float32
            ).astype(jnp.bfloat16)
            at = pl.ds(pl.multiple_of(b * size, size), size)
            for k in range(width // size):
                for p in range(aux):
                    halfway[half * (width // size) + k, at, p * size : (p + 1) * size] = product[
                        p * size : (p + 1) * size, k * size : (k + 1) * size
                    ]
            return carry

        for source in range(sources):
            if half == 0:
                own_copies[source].wait()
            lax.fori_loop(source * per_source, (source + 1) * per_source, first, 0, unroll=True)

    total[...] = jnp.zeros_like(total)
    last_copy.wait()

    def add_in(tensor, which):
        def second(b, carry):
            block = (b // per_source * CORES + which) * per_source + b % per_source
            rhs = stacked(tensor, b // per_source, b % per_source, aux, neigh)
            for r in range(0, rows, PIECE):
                product = jnp.dot(
                    halfway[block, r : r + PIECE], rhs, preferred_element_type=jnp.float32
                )
                for j in range(neigh):
                    total[pairs[block * neigh + j], r : r + PIECE] += product[
                        :, j * size : (j + 1) * size
                    ]
            return carry

        lax.fori_loop(0, sources * per_source, second, 0, unroll=4)

    add_in(own, core)
    add_in(other, 1 - core)

    out_ref[...] = jnp.zeros_like(out_ref)
    row = lax.broadcasted_iota(jnp.int32, (size, 2 * LANES), 0)
    column = lax.broadcasted_iota(jnp.int32, (size, 2 * LANES), 1)
    for n in range(blocks):
        chosen = (column == row + shifts[n]) & (row < counts[n])
        moved_columns = jnp.dot(
            total[n].astype(jnp.bfloat16),
            jnp.where(chosen, 1.0, 0.0).astype(jnp.bfloat16),
            preferred_element_type=jnp.float32,
        ).astype(jnp.bfloat16)
        at = pl.ds(pl.multiple_of(starts[n] * LANES, LANES), 2 * LANES)
        out_ref[:, at] += moved_columns


def exchange_rows(place, pairs, starts, shifts, counts, own, other, here_a, there_a, here_b, there_b):
    sources, aux, per_source, neigh, size, _ = own.shape
    width = here_a.shape[-1]
    blocks = 2 * width // size
    rows = sources * per_source * size
    scalar, vector = pl.BlockSpec(memory_space=pltpu.SMEM), pl.BlockSpec(memory_space=pltpu.VMEM)
    return pl.pallas_call(
        exchange_kernel,
        out_shape=jax.ShapeDtypeStruct((rows, LIVE), jnp.bfloat16),
        in_specs=[scalar] * 5 + [pl.BlockSpec(memory_space=pl.ANY)] * 6,
        out_specs=vector,
        scratch_shapes=[
            pltpu.VMEM(own.shape, jnp.bfloat16),
            pltpu.VMEM(own.shape, jnp.bfloat16),
            pltpu.VMEM((2, CORES) + here_a.shape, jnp.bfloat16),
            pltpu.VMEM((blocks, rows, aux * size), jnp.bfloat16),
            pltpu.VMEM((blocks, rows, size), jnp.float32),
            pltpu.SemaphoreType.DMA((sources + 5,)),
        ],
        compiler_params=pltpu.CompilerParams(vmem_limit_bytes=56 << 20),
        cost_estimate=pl.CostEstimate(
            flops=4 * rows * aux * neigh * size * blocks * size,
            bytes_accessed=4 * own.size + 8 * here_a.size + 2 * rows * LIVE,
            transcendentals=0,
        ),
    )(place, pairs, starts, shifts, counts, own, other, here_a, there_a, here_b, there_b)


def finish_kernel(rows_live, starts, shifts, counts, pieces, out_ref, summed):
    amount, rows, _ = pieces.shape
    summed[...] = jnp.zeros_like(summed)

    def add(i, carry):
        part = pieces[pl.ds(i * 8, 8)].astype(jnp.float32)
        summed[...] += jnp.sum(part, axis=0)
        return carry

    lax.fori_loop(0, amount // 8, add, 0)
    row = lax.broadcasted_iota(jnp.int32, (rows, LANES), 0)
    lane = lax.broadcasted_iota(jnp.int32, (rows, LANES), 1)
    for n in range(out_ref.shape[1] // LANES):
        window = summed[:, pl.ds(pl.multiple_of(starts[n] * LANES, LANES), 2 * LANES)]
        turned = pltpu.roll(window, lax.rem(2 * LANES - shifts[n], 2 * LANES), axis=1)
        live = (lane < counts[n]) & (row < rows_live[0])
        out_ref[:, n * LANES : (n + 1) * LANES] = jnp.where(live, turned[:, :LANES], 0.0)


def finish(rows_live, starts, shifts, counts, pieces, basis):
    rows = pieces.shape[1]
    scalar, vector = pl.BlockSpec(memory_space=pltpu.SMEM), pl.BlockSpec(memory_space=pltpu.VMEM)
    return pl.pallas_call(
        finish_kernel,
        out_shape=jax.ShapeDtypeStruct((rows, basis), jnp.float32),
        in_specs=[scalar] * 4 + [vector],
        out_specs=vector,
        scratch_shapes=[pltpu.VMEM((rows, LIVE), jnp.float32)],
    )(rows_live, starts, shifts, counts, pieces)


def moved(value, axis, shift):
    return lax.ppermute(value, axis, [(k, (k + shift) % SIDE) for k in range(SIDE)])


def swapped(value):
    return lax.ppermute(value, "core", [(0, 1), (1, 0)])


def ring(value, axis):
    up, down = moved(value, axis, 1), moved(value, axis, SIDE - 1)
    cut = value.shape[0] // 2
    far = [moved(up[:cut], axis, 1), moved(down[cut:], axis, SIDE - 1)]
    return jnp.stack([value, up, jnp.concatenate(far), down])


def per_device(three_index, density, pair_blocks, basis_counts):
    aux_here, own_blocks, neigh, size, _ = three_index.shape
    rows_here, basis = density.shape
    blocks = basis // size
    x, core, z, y = (lax.axis_index(name) for name in ("x", "core", "z", "y"))

    numbers = jnp.arange(blocks)
    offsets = jnp.sum(jnp.where(numbers[None, :] < numbers[:, None], basis_counts[None, :], 0), axis=1)
    starts = jnp.minimum(offsets // LANES, LIVE // LANES - 2)
    shifts = offsets - starts * LANES

    from_x = lax.rem(x - jnp.arange(SIDE) + SIDE, SIDE)
    first_row = (from_x * CORES + core) * own_blocks * size + (z * SIDE + y) * rows_here
    chosen = numbers[None, :] == (first_row // size)[:, None]
    rows_live = jnp.sum(jnp.where(chosen, basis_counts[None, :], 0), axis=1) - first_row % size
    column_live = (jnp.arange(size)[None, :] < basis_counts[:, None]).reshape(basis)
    live = (jnp.arange(rows_here)[None, :] < rows_live[:, None])[:, :, None] & column_live

    lines = jnp.stack([density] + [moved(density, "x", s) for s in range(1, SIDE)])
    lines = jnp.where(live, lines, 0)
    lines, three_index = lax.optimization_barrier((lines, three_index))
    here_a = ring(ring(lines[..., : basis // 2], "z"), "y")
    here_b = ring(ring(lines[..., basis // 2 :], "y"), "z")

    parted = three_index.reshape(SIDE, aux_here // SIDE, own_blocks, neigh, size, size)
    own = lax.all_to_all(parted, "x", 0, 0, tiled=True)
    own, here_a, here_b = lax.optimization_barrier((own, here_a, here_b))
    there_a, there_b, other = swapped(here_a), swapped(here_b), swapped(own)

    place = jnp.stack([x, core, z, y]).astype(jnp.int32)
    pairs = pair_blocks.reshape(-1)
    partial = exchange_rows(
        place, pairs, starts, shifts, basis_counts, own, other, here_a, there_a, here_b, there_b
    )
    partial = partial.reshape(-1, rows_here, LIVE)
    pieces = lax.all_to_all(partial, ("x", "z", "y"), 0, 0, tiled=True)
    still = rows_live[0].astype(jnp.int32).reshape(1)
    return finish(still, starts, shifts, basis_counts, pieces, basis)


def solution(mesh):
    devices = mesh.devices.reshape(SIDE, CORES, SIDE, SIDE)
    fine = Mesh(devices, ("x", "core", "z", "y"))
    in_specs = (P(("z", "y"), ("x", "core")), P(("x", "core", "z", "y"), None), P(), P())
    out_specs = P(("x", "core", "z", "y"), None)
    return jax.shard_map(
        per_device, mesh=fine, in_specs=in_specs, out_specs=out_specs, check_vma=False
    )
```

```python
import jax
import jax.numpy as jnp
from jax import lax
from jax.experimental import pallas as pl
from jax.experimental.pallas import tpu as pltpu
from jax.sharding import Mesh, PartitionSpec as P

CORES = 2
SIDE = 4
LIVE = 1536
LANES = 128
PIECE = 128


def stacked(tensor, source, mi, aux, neigh):
    return jnp.concatenate(
        [
            jnp.concatenate([tensor[source, p, mi, j] for j in range(neigh)], axis=1)
            for p in range(aux)
        ],
        axis=0,
    )


def exchange_kernel(place, pairs, starts, shifts, counts, own_hbm, other_hbm, here_a, here_b, *refs):
    there_a, there_b = refs[:SIDE], refs[SIDE : 2 * SIDE]
    out_ref, own, other, density, halfway, total, sems = refs[2 * SIDE :]
    sources, aux, per_source, neigh, size, _ = own.shape
    piece, width = density.shape[-2:]
    blocks, rows, _ = halfway.shape
    x, core, z, y = place[0], place[1], place[2], place[3]

    def copy(source, target, index):
        return pltpu.make_async_copy(source, target, sems.at[index])

    own_copies = [copy(own_hbm.at[s], own.at[s], s) for s in range(sources)]
    def density_copies(half, here, there, index):
        copies = [copy(here, density.at[half, 0], index)]
        for back in range(SIDE):
            copies.append(copy(there[back], density.at[half, 1, back], index + 1 + back))
        return copies

    first_copies = density_copies(0, here_a, there_a, sources)
    next_copies = density_copies(1, here_b, there_b, sources + SIDE + 1)
    last_copy = copy(other_hbm, other, sources + 2 * SIDE + 2)
    for one in own_copies[:1] + first_copies:
        one.start()
    for one in first_copies:
        one.wait()
    for one in own_copies[1:] + next_copies:
        one.start()
    last_copy.start()

    for half in range(2):
        if half == 1:
            for one in next_copies:
                one.wait()

        def first(b, carry):
            source, mi = b // per_source, b % per_source
            block = (source * CORES + core) * per_source + mi
            lhs = stacked(own, source, mi, aux, neigh)
            near = []
            for j in range(neigh):
                partner = pairs[block * neigh + j]
                back_x = lax.rem(x - partner // (CORES * per_source) + SIDE, SIDE)
                swap = jnp.where(partner // per_source % CORES == core, 0, 1)
                for zy in range(size // piece):
                    from_z = partner % per_source * (SIDE // per_source) + zy // SIDE
                    back_z = lax.rem(z - from_z + SIDE, SIDE)
                    back_y = lax.rem(y - zy % SIDE + SIDE, SIDE)
                    outer, inner = (back_y, back_z) if half == 0 else (back_z, back_y)
                    near.append(density[half, swap, outer, inner, back_x])
            product = jnp.dot(
                lhs, jnp.concatenate(near, axis=0), preferred_element_type=jnp.float32
            ).astype(jnp.bfloat16)
            at = pl.ds(pl.multiple_of(b * size, size), size)
            for k in range(width // size):
                for p in range(aux):
                    halfway[half * (width // size) + k, at, p * size : (p + 1) * size] = product[
                        p * size : (p + 1) * size, k * size : (k + 1) * size
                    ]
            return carry

        for source in range(sources):
            if half == 0:
                own_copies[source].wait()
            lax.fori_loop(source * per_source, (source + 1) * per_source, first, 0, unroll=True)

    total[...] = jnp.zeros_like(total)
    last_copy.wait()

    def add_in(tensor, which):
        def second(b, carry):
            block = (b // per_source * CORES + which) * per_source + b % per_source
            rhs = stacked(tensor, b // per_source, b % per_source, aux, neigh)
            for r in range(0, rows, PIECE):
                product = jnp.dot(
                    halfway[block, r : r + PIECE], rhs, preferred_element_type=jnp.float32
                )
                for j in range(neigh):
                    total[pairs[block * neigh + j], r : r + PIECE] += product[
                        :, j * size : (j + 1) * size
                    ]
            return carry

        lax.fori_loop(0, sources * per_source, second, 0, unroll=4)

    add_in(own, core)
    add_in(other, 1 - core)

    out_ref[...] = jnp.zeros_like(out_ref)
    row = lax.broadcasted_iota(jnp.int32, (size, 2 * LANES), 0)
    column = lax.broadcasted_iota(jnp.int32, (size, 2 * LANES), 1)
    for n in range(blocks):
        chosen = (column == row + shifts[n]) & (row < counts[n])
        moved_columns = jnp.dot(
            total[n].astype(jnp.bfloat16),
            jnp.where(chosen, 1.0, 0.0).astype(jnp.bfloat16),
            preferred_element_type=jnp.float32,
        ).astype(jnp.bfloat16)
        at = pl.ds(pl.multiple_of(starts[n] * LANES, LANES), 2 * LANES)
        out_ref[:, at] += moved_columns


def exchange_rows(place, pairs, starts, shifts, counts, own, other, here_a, here_b, there_a, there_b):
    sources, aux, per_source, neigh, size, _ = own.shape
    width = here_a.shape[-1]
    blocks = 2 * width // size
    rows = sources * per_source * size
    scalar, vector = pl.BlockSpec(memory_space=pltpu.SMEM), pl.BlockSpec(memory_space=pltpu.VMEM)
    return pl.pallas_call(
        exchange_kernel,
        out_shape=jax.ShapeDtypeStruct((rows, LIVE), jnp.bfloat16),
        in_specs=[scalar] * 5 + [pl.BlockSpec(memory_space=pl.ANY)] * (4 + 2 * SIDE),
        out_specs=vector,
        scratch_shapes=[
            pltpu.VMEM(own.shape, jnp.bfloat16),
            pltpu.VMEM(own.shape, jnp.bfloat16),
            pltpu.VMEM((2, CORES) + here_a.shape, jnp.bfloat16),
            pltpu.VMEM((blocks, rows, aux * size), jnp.bfloat16),
            pltpu.VMEM((blocks, rows, size), jnp.float32),
            pltpu.SemaphoreType.DMA((sources + 2 * SIDE + 3,)),
        ],
        compiler_params=pltpu.CompilerParams(vmem_limit_bytes=56 << 20),
        cost_estimate=pl.CostEstimate(
            flops=4 * rows * aux * neigh * size * blocks * size,
            bytes_accessed=4 * own.size + 8 * here_a.size + 2 * rows * LIVE,
            transcendentals=0,
        ),
    )(place, pairs, starts, shifts, counts, own, other, here_a, here_b, *there_a, *there_b)


def finish_kernel(rows_live, starts, shifts, counts, pieces, out_ref, summed):
    amount, rows, _ = pieces.shape
    summed[...] = jnp.zeros_like(summed)

    def add(i, carry):
        part = pieces[pl.ds(i * 8, 8)].astype(jnp.float32)
        summed[...] += jnp.sum(part, axis=0)
        return carry

    lax.fori_loop(0, amount // 8, add, 0)
    row = lax.broadcasted_iota(jnp.int32, (rows, LANES), 0)
    lane = lax.broadcasted_iota(jnp.int32, (rows, LANES), 1)
    for n in range(out_ref.shape[1] // LANES):
        window = summed[:, pl.ds(pl.multiple_of(starts[n] * LANES, LANES), 2 * LANES)]
        turned = pltpu.roll(window, lax.rem(2 * LANES - shifts[n], 2 * LANES), axis=1)
        live = (lane < counts[n]) & (row < rows_live[0])
        out_ref[:, n * LANES : (n + 1) * LANES] = jnp.where(live, turned[:, :LANES], 0.0)


def finish(rows_live, starts, shifts, counts, pieces, basis):
    rows = pieces.shape[1]
    scalar, vector = pl.BlockSpec(memory_space=pltpu.SMEM), pl.BlockSpec(memory_space=pltpu.VMEM)
    return pl.pallas_call(
        finish_kernel,
        out_shape=jax.ShapeDtypeStruct((rows, basis), jnp.float32),
        in_specs=[scalar] * 4 + [vector],
        out_specs=vector,
        scratch_shapes=[pltpu.VMEM((rows, LIVE), jnp.float32)],
    )(rows_live, starts, shifts, counts, pieces)


def moved(value, axis, shift):
    return lax.ppermute(value, axis, [(k, (k + shift) % SIDE) for k in range(SIDE)])


def swapped(value):
    return lax.ppermute(value, "core", [(0, 1), (1, 0)])


def ring(value, axis):
    up, down = moved(value, axis, 1), moved(value, axis, SIDE - 1)
    cut = value.shape[0] // 2
    far = [moved(up[:cut], axis, 1), moved(down[cut:], axis, SIDE - 1)]
    return jnp.stack([value, up, jnp.concatenate(far), down])


def last_ring(value, axis):
    up, down = moved(value, axis, 1), moved(value, axis, SIDE - 1)
    cut = value.shape[0] // 2
    far = jnp.concatenate([moved(up[:cut], axis, 1), moved(down[cut:], axis, SIDE - 1)])
    return jnp.stack([value, up, far, down]), far, (swapped(value), swapped(up), swapped(down))


def per_device(three_index, density, pair_blocks, basis_counts):
    aux_here, own_blocks, neigh, size, _ = three_index.shape
    rows_here, basis = density.shape
    blocks = basis // size
    x, core, z, y = (lax.axis_index(name) for name in ("x", "core", "z", "y"))

    numbers = jnp.arange(blocks)
    offsets = jnp.sum(jnp.where(numbers[None, :] < numbers[:, None], basis_counts[None, :], 0), axis=1)
    starts = jnp.minimum(offsets // LANES, LIVE // LANES - 2)
    shifts = offsets - starts * LANES

    from_x = lax.rem(x - jnp.arange(SIDE) + SIDE, SIDE)
    first_row = (from_x * CORES + core) * own_blocks * size + (z * SIDE + y) * rows_here
    chosen = numbers[None, :] == (first_row // size)[:, None]
    rows_live = jnp.sum(jnp.where(chosen, basis_counts[None, :], 0), axis=1) - first_row % size
    column_live = (jnp.arange(size)[None, :] < basis_counts[:, None]).reshape(basis)
    live = (jnp.arange(rows_here)[None, :] < rows_live[:, None])[:, :, None] & column_live

    lines = jnp.stack([density] + [moved(density, "x", s) for s in range(1, SIDE)])
    lines = jnp.where(live, lines, 0)
    lines, three_index = lax.optimization_barrier((lines, three_index))
    here_a, far_a, near_a = last_ring(ring(lines[..., : basis // 2], "z"), "y")
    here_b, far_b, near_b = last_ring(ring(lines[..., basis // 2 :], "y"), "z")

    parted = three_index.reshape(SIDE, aux_here // SIDE, own_blocks, neigh, size, size)
    own = lax.all_to_all(parted, "x", 0, 0, tiled=True)
    own, here_a, here_b, far_a, far_b, near_a, near_b = lax.optimization_barrier(
        (own, here_a, here_b, far_a, far_b, near_a, near_b)
    )
    there_a = (near_a[0], near_a[1], swapped(far_a), near_a[2])
    there_b = (near_b[0], near_b[1], swapped(far_b), near_b[2])
    other = swapped(own)

    place = jnp.stack([x, core, z, y]).astype(jnp.int32)
    pairs = pair_blocks.reshape(-1)
    partial = exchange_rows(
        place, pairs, starts, shifts, basis_counts, own, other, here_a, here_b, there_a, there_b
    )
    partial = partial.reshape(-1, rows_here, LIVE)
    pieces = lax.all_to_all(partial, ("x", "z", "y"), 0, 0, tiled=True)
    still = rows_live[0].astype(jnp.int32).reshape(1)
    return finish(still, starts, shifts, basis_counts, pieces, basis)


def solution(mesh):
    devices = mesh.devices.reshape(SIDE, CORES, SIDE, SIDE)
    fine = Mesh(devices, ("x", "core", "z", "y"))
    in_specs = (P(("z", "y"), ("x", "core")), P(("x", "core", "z", "y"), None), P(), P())
    out_specs = P(("x", "core", "z", "y"), None)
    return jax.shard_map(
        per_device, mesh=fine, in_specs=in_specs, out_specs=out_specs, check_vma=False
    )
```

```python
import jax
import jax.numpy as jnp
from jax import lax
from jax.experimental import pallas as pl
from jax.experimental.pallas import tpu as pltpu
from jax.sharding import Mesh, PartitionSpec as P

CORES = 2
SIDE = 4
LIVE = 1536
LANES = 128
PIECE = 128


def stacked(tensor, source, mi, aux, neigh):
    return jnp.concatenate(
        [
            jnp.concatenate([tensor[source, p, mi, j] for j in range(neigh)], axis=1)
            for p in range(aux)
        ],
        axis=0,
    )


def exchange_kernel(place, pairs, starts, shifts, counts, own_hbm, other_hbm, *refs):
    here_a, here_b = refs[:SIDE], refs[SIDE : 2 * SIDE]
    there_a, there_b = refs[2 * SIDE : 3 * SIDE], refs[3 * SIDE : 4 * SIDE]
    out_ref, own, other, density, halfway, total, sems = refs[4 * SIDE :]
    sources, aux, per_source, neigh, size, _ = own.shape
    piece, width = density.shape[-2:]
    blocks, rows, _ = halfway.shape
    x, core, z, y = place[0], place[1], place[2], place[3]

    def copy(source, target, index):
        return pltpu.make_async_copy(source, target, sems.at[index])

    own_copies = [copy(own_hbm.at[s], own.at[s], s) for s in range(sources)]
    def density_copies(half, here, there, index):
        copies = []
        for back in range(SIDE):
            copies.append(copy(here[back], density.at[half, 0, back], index + back))
            copies.append(copy(there[back], density.at[half, 1, back], index + SIDE + back))
        return copies

    first_copies = density_copies(0, here_a, there_a, sources)
    next_copies = density_copies(1, here_b, there_b, sources + 2 * SIDE)
    last_copy = copy(other_hbm, other, sources + 4 * SIDE)
    for one in own_copies[:1] + first_copies:
        one.start()
    for one in first_copies:
        one.wait()
    for one in own_copies[1:] + next_copies:
        one.start()
    last_copy.start()

    for half in range(2):
        if half == 1:
            for one in next_copies:
                one.wait()

        def first(b, carry):
            source, mi = b // per_source, b % per_source
            block = (source * CORES + core) * per_source + mi
            lhs = stacked(own, source, mi, aux, neigh)
            near = []
            for j in range(neigh):
                partner = pairs[block * neigh + j]
                back_x = lax.rem(x - partner // (CORES * per_source) + SIDE, SIDE)
                swap = jnp.where(partner // per_source % CORES == core, 0, 1)
                for zy in range(size // piece):
                    from_z = partner % per_source * (SIDE // per_source) + zy // SIDE
                    back_z = lax.rem(z - from_z + SIDE, SIDE)
                    back_y = lax.rem(y - zy % SIDE + SIDE, SIDE)
                    outer, inner = (back_y, back_z) if half == 0 else (back_z, back_y)
                    near.append(density[half, swap, outer, inner, back_x])
            product = jnp.dot(
                lhs, jnp.concatenate(near, axis=0), preferred_element_type=jnp.float32
            ).astype(jnp.bfloat16)
            at = pl.ds(pl.multiple_of(b * size, size), size)
            for k in range(width // size):
                for p in range(aux):
                    halfway[half * (width // size) + k, at, p * size : (p + 1) * size] = product[
                        p * size : (p + 1) * size, k * size : (k + 1) * size
                    ]
            return carry

        for source in range(sources):
            if half == 0:
                own_copies[source].wait()
            lax.fori_loop(source * per_source, (source + 1) * per_source, first, 0, unroll=True)

    total[...] = jnp.zeros_like(total)
    last_copy.wait()

    def add_in(tensor, which):
        def second(b, carry):
            block = (b // per_source * CORES + which) * per_source + b % per_source
            rhs = stacked(tensor, b // per_source, b % per_source, aux, neigh)
            for r in range(0, rows, PIECE):
                product = jnp.dot(
                    halfway[block, r : r + PIECE], rhs, preferred_element_type=jnp.float32
                )
                for j in range(neigh):
                    total[pairs[block * neigh + j], r : r + PIECE] += product[
                        :, j * size : (j + 1) * size
                    ]
            return carry

        lax.fori_loop(0, sources * per_source, second, 0, unroll=4)

    add_in(own, core)
    add_in(other, 1 - core)

    out_ref[...] = jnp.zeros_like(out_ref)
    row = lax.broadcasted_iota(jnp.int32, (size, 2 * LANES), 0)
    column = lax.broadcasted_iota(jnp.int32, (size, 2 * LANES), 1)
    for n in range(blocks):
        chosen = (column == row + shifts[n]) & (row < counts[n])
        moved_columns = jnp.dot(
            total[n].astype(jnp.bfloat16),
            jnp.where(chosen, 1.0, 0.0).astype(jnp.bfloat16),
            preferred_element_type=jnp.float32,
        ).astype(jnp.bfloat16)
        at = pl.ds(pl.multiple_of(starts[n] * LANES, LANES), 2 * LANES)
        out_ref[:, at] += moved_columns


def exchange_rows(place, pairs, starts, shifts, counts, own, other, here_a, here_b, there_a, there_b):
    sources, aux, per_source, neigh, size, _ = own.shape
    width = here_a[0].shape[-1]
    blocks = 2 * width // size
    rows = sources * per_source * size
    scalar, vector = pl.BlockSpec(memory_space=pltpu.SMEM), pl.BlockSpec(memory_space=pltpu.VMEM)
    return pl.pallas_call(
        exchange_kernel,
        out_shape=jax.ShapeDtypeStruct((rows, LIVE), jnp.bfloat16),
        in_specs=[scalar] * 5 + [pl.BlockSpec(memory_space=pl.ANY)] * (2 + 4 * SIDE),
        out_specs=vector,
        scratch_shapes=[
            pltpu.VMEM(own.shape, jnp.bfloat16),
            pltpu.VMEM(own.shape, jnp.bfloat16),
            pltpu.VMEM((2, CORES, SIDE) + here_a[0].shape, jnp.bfloat16),
            pltpu.VMEM((blocks, rows, aux * size), jnp.bfloat16),
            pltpu.VMEM((blocks, rows, size), jnp.float32),
            pltpu.SemaphoreType.DMA((sources + 4 * SIDE + 1,)),
        ],
        compiler_params=pltpu.CompilerParams(vmem_limit_bytes=56 << 20),
        cost_estimate=pl.CostEstimate(
            flops=4 * rows * aux * neigh * size * blocks * size,
            bytes_accessed=4 * own.size + 8 * SIDE * here_a[0].size + 2 * rows * LIVE,
            transcendentals=0,
        ),
    )(place, pairs, starts, shifts, counts, own, other, *here_a, *here_b, *there_a, *there_b)


def finish_kernel(rows_live, starts, shifts, counts, pieces, out_ref, summed):
    _, rows, _ = pieces.shape
    step = pl.program_id(0)
    part = jnp.sum(pieces[...].astype(jnp.float32), axis=0)

    @pl.when(step == 0)
    def _():
        summed[...] = part

    @pl.when(step > 0)
    def _():
        summed[...] += part

    @pl.when(step == pl.num_programs(0) - 1)
    def _():
        row = lax.broadcasted_iota(jnp.int32, (rows, LANES), 0)
        lane = lax.broadcasted_iota(jnp.int32, (rows, LANES), 1)
        for n in range(out_ref.shape[1] // LANES):
            window = summed[:, pl.ds(pl.multiple_of(starts[n] * LANES, LANES), 2 * LANES)]
            turned = pltpu.roll(window, lax.rem(2 * LANES - shifts[n], 2 * LANES), axis=1)
            live = (lane < counts[n]) & (row < rows_live[0])
            out_ref[:, n * LANES : (n + 1) * LANES] = jnp.where(live, turned[:, :LANES], 0.0)


def finish(rows_live, starts, shifts, counts, pieces, basis, steps=8):
    amount, rows, _ = pieces.shape
    return pl.pallas_call(
        finish_kernel,
        out_shape=jax.ShapeDtypeStruct((rows, basis), jnp.float32),
        grid=(steps,),
        in_specs=[pl.BlockSpec(memory_space=pltpu.SMEM)] * 4
        + [pl.BlockSpec((amount // steps, rows, LIVE), lambda i: (i, 0, 0))],
        out_specs=pl.BlockSpec((rows, basis), lambda i: (0, 0)),
        scratch_shapes=[pltpu.VMEM((rows, LIVE), jnp.float32)],
    )(rows_live, starts, shifts, counts, pieces)


def moved(value, axis, shift):
    return lax.ppermute(value, axis, [(k, (k + shift) % SIDE) for k in range(SIDE)])


def swapped(value):
    return lax.ppermute(value, "core", [(0, 1), (1, 0)])


def ring(value, axis):
    up, down = moved(value, axis, 1), moved(value, axis, SIDE - 1)
    cut = value.shape[0] // 2
    far = [moved(up[:cut], axis, 1), moved(down[cut:], axis, SIDE - 1)]
    return jnp.stack([value, up, jnp.concatenate(far), down])


def last_ring(value, axis):
    up, down = moved(value, axis, 1), moved(value, axis, SIDE - 1)
    cut = value.shape[0] // 2
    far = jnp.concatenate([moved(up[:cut], axis, 1), moved(down[cut:], axis, SIDE - 1)])
    here = (value, up, far, down)
    return here, tuple(swapped(block) for block in here)


def per_device(three_index, density, pair_blocks, basis_counts):
    aux_here, own_blocks, neigh, size, _ = three_index.shape
    rows_here, basis = density.shape
    blocks = basis // size
    x, core, z, y = (lax.axis_index(name) for name in ("x", "core", "z", "y"))

    numbers = jnp.arange(blocks)
    offsets = jnp.sum(jnp.where(numbers[None, :] < numbers[:, None], basis_counts[None, :], 0), axis=1)
    starts = jnp.minimum(offsets // LANES, LIVE // LANES - 2)
    shifts = offsets - starts * LANES

    from_x = lax.rem(x - jnp.arange(SIDE) + SIDE, SIDE)
    first_row = (from_x * CORES + core) * own_blocks * size + (z * SIDE + y) * rows_here
    chosen = numbers[None, :] == (first_row // size)[:, None]
    rows_live = jnp.sum(jnp.where(chosen, basis_counts[None, :], 0), axis=1) - first_row % size
    column_live = (jnp.arange(size)[None, :] < basis_counts[:, None]).reshape(basis)
    live = (jnp.arange(rows_here)[None, :] < rows_live[:, None])[:, :, None] & column_live

    lines = jnp.stack([density] + [moved(density, "x", s) for s in range(1, SIDE)])
    lines = jnp.where(live, lines, 0)
    lines, three_index = lax.optimization_barrier((lines, three_index))
    here_a, there_a = last_ring(ring(lines[..., : basis // 2], "z"), "y")
    here_b, there_b = last_ring(ring(lines[..., basis // 2 :], "y"), "z")

    parted = three_index.reshape(SIDE, aux_here // SIDE, own_blocks, neigh, size, size)
    own = lax.all_to_all(parted, "x", 0, 0, tiled=True)
    own, there_a, there_b = lax.optimization_barrier((own, there_a, there_b))
    other = swapped(own)

    place = jnp.stack([x, core, z, y]).astype(jnp.int32)
    pairs = pair_blocks.reshape(-1)
    partial = exchange_rows(
        place, pairs, starts, shifts, basis_counts, own, other, here_a, here_b, there_a, there_b
    )
    partial = partial.reshape(-1, rows_here, LIVE)
    pieces = lax.all_to_all(partial, ("x", "z", "y"), 0, 0, tiled=True)
    still = rows_live[0].astype(jnp.int32).reshape(1)
    return finish(still, starts, shifts, basis_counts, pieces, basis)


def solution(mesh):
    devices = mesh.devices.reshape(SIDE, CORES, SIDE, SIDE)
    fine = Mesh(devices, ("x", "core", "z", "y"))
    in_specs = (P(("z", "y"), ("x", "core")), P(("x", "core", "z", "y"), None), P(), P())
    out_specs = P(("x", "core", "z", "y"), None)
    return jax.shard_map(
        per_device, mesh=fine, in_specs=in_specs, out_specs=out_specs, check_vma=False
    )
```
